256 devices in a mesh: site: 8 (over x, y_lo), blk: 32 (over y_hi, z, core).
Axes of the slice: x: 4, y: 4 (y_hi: 2, y_lo: 2; y = y_hi * 2 + y_lo), z: 8, core: 2. Of those that a mesh axis runs over, the one named last changes fastest.
Arguments:
- corner: bfloat16 [8, 768, 768], P('site', 'blk'), may hold values from -6 to 6
- edge: bfloat16 [8, 768, 64, 768], P('site', 'blk'), may hold values from -0.02734375 to 0.02734375
- proj_left: bfloat16 [8, 768, 64, 768], P('site', 'blk'), may hold values from -0.21875 to 0.21875
- proj_right: bfloat16 [8, 768, 64, 768], P('site', 'blk'), may hold values from -0.21875 to 0.21875
- charge: int32 [8, 768], P('site'), may hold values from 0 to 15, never falling along the last dimension, each value on 1 to 96 neighbouring positions
- cot_left: float32 [8, 768, 768], P('site', 'blk'), may hold values from -2 to 2
- cot_right: float32 [8, 768, 768], P('site', 'blk'), may hold values from -2 to 2
Outputs:
- new_left: bfloat16 [8, 768, 768], P('site', 'blk')
- new_right: bfloat16 [8, 768, 768], P('site', 'blk')
- grad_left: bfloat16 [8, 768, 64, 768], P('site', 'blk')
- grad_right: bfloat16 [8, 768, 64, 768], P('site', 'blk')
The draws below stay inside these ranges and needn't reach their ends.
Inputs may be any that keep to these rules, and one draw needn't show every extreme that they name: `charge`: sector labels never fall along the bond index; each sector holds 1 to 96 indices.
All inputs are finite; a program needn't handle non-finite values.
Results may differ from the reference program's by a relative error of at most 0.0059.
Values may be sent and summed in bfloat16 or wider, within the bound.
No kernel may reach another device: no remote copies, remote signals or barrier semaphores. Data moves between devices by JAX's collectives and lax.ppermute only.
A program may use at most 64 MiB of HBM per device.

```python
import math
import jax
import jax.numpy as jnp
import numpy as np
from jax import lax

CHI = 768
DD = 64
NSEC = 16
ITERS = 2
SITES = 8


def block_scale(key, shape, shards, least, largest):
    level = 1.0
    for axis_at, parts in shards:
        heights = jax.random.uniform(jax.random.fold_in(jax.random.fold_in(key, 6), axis_at), (parts,), jnp.float32, least / len(shards), largest / len(shards))
        level = level * jnp.repeat(jnp.exp(heights), shape[axis_at] // parts).reshape((-1,) + (1,) * (len(shape) - 1 - axis_at))
    return level


def profile(number_of, total, limit, skew):
    loads = [(1 << 20) // math.isqrt(rank ** skew) + 1 for rank in range(2, number_of + 1)]
    spare, holding = total - limit - (number_of - 1), [1] * (number_of - 1)
    while spare > 0:
        free = [i for i in range(number_of - 1) if holding[i] < limit]
        whole, budget = sum([loads[i] for i in free]), spare
        for i in free:
            more = min(limit - holding[i], max(1, budget * loads[i] // whole), spare)
            holding[i] = holding[i] + more
            spare = spare - more
    return np.array([limit] + holding)


def ragged(own_key, count, total, bound, skew):
    if count == 2:
        one = jax.random.randint(own_key, (), max(1, total - bound), min(bound, total - 1) + 1)
        return jnp.stack([one, total - one])
    tallies = jnp.asarray(profile(count, total, bound, skew), jnp.int32)
    pairs = (count - 1) // 2
    giver, taker = tallies[1:1 + 2 * pairs:2], tallies[2:2 + 2 * pairs:2]
    room = jnp.minimum(giver - 1, bound - taker)
    passed = jax.random.randint(jax.random.fold_in(own_key, 1), (pairs,), 0, 1 << 20) % (room + 1)
    tallies = tallies.at[1:1 + 2 * pairs:2].set(giver - passed).at[2:2 + 2 * pairs:2].set(taker + passed)
    return tallies[jax.random.permutation(jax.random.fold_in(own_key, 2), count)]


def centred(rng, dims, deviation, limit, pieces=(), dtype=jnp.bfloat16):
    factor_of = block_scale(rng, dims, pieces, -0.22, 0.18) if pieces else 1.0
    drawn = jax.random.normal(rng, dims, jnp.float32) * deviation * factor_of
    return jnp.minimum(jnp.maximum(drawn, -limit), limit).astype(dtype)


def setup_inputs(seed: int = 0) -> dict:
    splits = jax.random.split(jax.random.key(seed), 8)
    corner = centred(splits[0], (SITES, CHI, CHI), 1.0, 6.0, ((0, 8), (1, 32)))
    edge = centred(splits[1], (SITES, CHI, DD, CHI), (CHI * DD) ** -0.5, 0.02734375, ((0, 8), (1, 32)))
    proj_left = centred(splits[2], (SITES, CHI, DD, CHI), CHI ** -0.5, 0.21875, ((0, 8), (1, 32)))
    proj_right = centred(splits[3], (SITES, CHI, DD, CHI), CHI ** -0.5, 0.21875, ((0, 8), (1, 32)))
    charge = jax.vmap(lambda own: jnp.searchsorted(jnp.cumsum(ragged(own, NSEC, CHI, CHI // 8, 2)), jnp.arange(CHI), side="right"))(jax.random.split(splits[4], SITES)).reshape((SITES, CHI)).astype(jnp.int32)
    cot_left = centred(splits[5], (SITES, CHI, CHI), 0.25, 2.0, ((0, 8), (1, 32)), jnp.float32)
    cot_right = centred(splits[6], (SITES, CHI, CHI), 0.25, 2.0, ((0, 8), (1, 32)), jnp.float32)
    return dict(corner=corner, edge=edge, proj_left=proj_left, proj_right=proj_right, charge=charge, cot_left=cot_left, cot_right=cot_right)


def contract_first(left, right):
    return lax.dot_general(left, right, (((0,), (0,)), ((), ())), preferred_element_type=jnp.float32)


def contract_last(left, right):
    return lax.dot_general(left, right, (((1,), (1,)), ((), ())), preferred_element_type=jnp.float32)


def reference(corner, edge, proj_left, proj_right, charge, cot_left, cot_right):
    count_sites = corner.shape[0]
    prev_corner = jnp.roll(corner, 1, axis=0)
    next_corner = jnp.roll(corner, -1, axis=0)
    mask = (charge[:, :, None] == charge[:, None, :]).astype(jnp.float32)
    edge_flat = edge.reshape(count_sites, CHI * DD, CHI)
    left_flat = proj_left.reshape(count_sites, CHI * DD, CHI)
    right_flat = proj_right.reshape(count_sites, CHI * DD, CHI)
    enl_left = jnp.stack([contract_first(edge_flat[s], left_flat[s]).astype(jnp.bfloat16) for s in range(count_sites)])
    enl_right = jnp.stack([contract_first(edge_flat[s], right_flat[s]).astype(jnp.bfloat16) for s in range(count_sites)])
    new_left = jnp.stack([(mask[s] * jnp.dot(prev_corner[s], enl_left[s], preferred_element_type=jnp.float32)).astype(jnp.bfloat16) for s in range(count_sites)])
    new_right = jnp.stack([(mask[s] * jnp.dot(next_corner[s], enl_right[s], preferred_element_type=jnp.float32)).astype(jnp.bfloat16) for s in range(count_sites)])
    adj_left = cot_left
    adj_right = cot_right
    for step in range(ITERS):
        w_left = (mask * adj_left).astype(jnp.bfloat16)
        w_right = (mask * adj_right).astype(jnp.bfloat16)
        back_left = jnp.stack([contract_last(w_left[s], enl_left[s]) for s in range(count_sites)])
        back_right = jnp.stack([contract_last(w_right[s], enl_right[s]) for s in range(count_sites)])
        adj_left = cot_left + jnp.roll(back_left, -1, axis=0)
        adj_right = cot_right + jnp.roll(back_right, 1, axis=0)
    w_left = (mask * adj_left).astype(jnp.bfloat16)
    w_right = (mask * adj_right).astype(jnp.bfloat16)
    grads_left = []
    grads_right = []
    for s in range(count_sites):
        mid_left = contract_first(prev_corner[s], w_left[s]).astype(jnp.bfloat16)
        mid_right = contract_first(next_corner[s], w_right[s]).astype(jnp.bfloat16)
        grads_left.append(jnp.dot(edge_flat[s], mid_left, preferred_element_type=jnp.float32).astype(jnp.bfloat16).reshape(CHI, DD, CHI))
        grads_right.append(jnp.dot(edge_flat[s], mid_right, preferred_element_type=jnp.float32).astype(jnp.bfloat16).reshape(CHI, DD, CHI))
    return new_left, new_right, jnp.stack(grads_left), jnp.stack(grads_right)
```

```python
import jax
import jax.numpy as jnp
from jax import lax
from jax.sharding import PartitionSpec as P

ITERS = 2
SECTORS = 16
FOLD = 128
WIDE = 384
F32 = jnp.float32
BF16 = jnp.bfloat16


def contract_first(left, right):
    return lax.dot_general(left, right, (((0,), (0,)), ((), ())), preferred_element_type=F32)


def contract_last(left, right):
    return lax.dot_general(left, right, (((1,), (1,)), ((), ())), preferred_element_type=F32)


def fold_lanes(x, width):
    pieces = [x[:, at : at + width] for at in range(0, x.shape[1], width)]
    total = pieces[0]
    for piece in pieces[1:]:
        total = total + piece
    return total


def body(corner, edge, proj_left, proj_right, charge, cot_left, cot_right):
    sites = lax.axis_size("site")
    members = lax.axis_size("blk")
    rows, chi = corner.shape[1], corner.shape[2]
    depth = edge.shape[2]
    chips = members // 2
    pair_rows = 2 * rows
    blk = lax.axis_index("blk")
    first = blk % 2 == 0
    chip = blk // 2
    groups = [[2 * q + core for q in range(chips)] for core in range(2)]

    def swap_cores(x):
        return lax.ppermute(x, "blk", [(i, i ^ 1) for i in range(members)])

    def site_move(x, distance, cross):
        route = []
        for s in range(sites):
            for i in range(members):
                target = i ^ 1 if cross else i
                sign = 1 if target % 2 == 0 else -1
                route.append((s * members + i, ((s + sign * distance) % sites) * members + target))
        return lax.ppermute(x, ("site", "blk"), route)

    def exchange(x):
        return lax.all_to_all(x, "blk", 0, 0, tiled=True, axis_index_groups=groups)

    def spread(x):
        return jnp.broadcast_to(x[None], (chips,) + x.shape)

    def pick(a, b):
        return jnp.where(first, a, b)

    def weave(own, other):
        halves = jnp.stack([pick(own, other), pick(other, own)], axis=1)
        return halves.reshape(chi, own.shape[-1])

    label = charge[0]
    label_to = site_move(charge, 1, False)[0]
    row_label = lax.dynamic_slice_in_dim(label, blk * rows, rows, 0)
    row_mask = row_label[:, None] == label[None, :]
    here = corner[0]
    start_left = fold_lanes(jnp.where(row_mask, cot_left[0], 0.0), FOLD).astype(BF16)
    start_right = fold_lanes(jnp.where(row_mask, cot_right[0], 0.0), FOLD).astype(BF16)
    early = exchange(spread(jnp.concatenate([here, start_left, start_right], axis=1)))

    edge_flat = edge[0].reshape(rows * depth, chi)
    part_left = contract_first(edge_flat, proj_left[0].reshape(rows * depth, chi))
    part_right = contract_first(edge_flat, proj_right[0].reshape(rows * depth, chi))
    other_part = swap_cores(pick(part_right, part_left).astype(BF16))
    part = pick(part_left, part_right) + other_part.astype(F32)
    part_bf = part.astype(BF16)

    sector = jnp.arange(SECTORS, dtype=jnp.int32)
    in_sector = label_to[None, :] == sector[:, None]
    least = jnp.min(jnp.where(in_sector, label[None, :], SECTORS), axis=1)
    most = jnp.max(jnp.where(in_sector, label[None, :], -1), axis=1)
    low = jnp.sum(jnp.where(label_to[:, None] == sector[None, :], least[None, :], 0), axis=1)
    high = jnp.sum(jnp.where(label_to[:, None] == sector[None, :], most[None, :], 0), axis=1)
    reach = (label[None, :] >= low[:, None]) & (label[None, :] <= high[:, None])
    narrow = fold_lanes(jnp.where(reach, part, 0.0), WIDE).astype(BF16)
    got = exchange(narrow.reshape(chips, pair_rows, WIDE))
    enl = jnp.sum(got.astype(F32), axis=0).astype(BF16)

    half = early[:, :, :chi]
    near = weave(site_move(half, 1, False), site_move(half, 1, True))
    early_left = early[:, :, chi : chi + FOLD]
    early_right = early[:, :, chi + FOLD :]
    w0 = weave(pick(early_left, early_right), swap_cores(pick(early_right, early_left)))

    same = label[:, None] == label[None, :]
    mine = lax.dynamic_slice_in_dim(label, chip * pair_rows, pair_rows, 0)
    mine_to = lax.dynamic_slice_in_dim(label_to, chip * pair_rows, pair_rows, 0)
    at_lane = (chip * pair_rows + jnp.arange(pair_rows, dtype=jnp.int32)) % FOLD
    select = (at_lane[:, None] == jnp.arange(FOLD, dtype=jnp.int32)[None, :]).astype(BF16)
    turned = contract_last(select, w0)
    cot_turned = fold_lanes(jnp.where(mine[:, None] == label[None, :], turned, 0.0), FOLD).astype(BF16)
    cot_to = site_move(cot_turned, 1, False).astype(F32)
    mask_to = mine_to[:, None] == label_to[None, :]

    def next_w(back):
        adj = cot_to + fold_lanes(jnp.where(mask_to, back, 0.0), FOLD)
        return site_move(adj.astype(BF16), -1, False)

    wide_mask = same[:, :WIDE] | same[:, WIDE:]
    w0_wide = jnp.where(wide_mask, jnp.concatenate([w0] * (WIDE // FOLD), axis=1), 0.0)
    w1 = next_w(contract_last(enl, w0_wide))
    w1_all = exchange(spread(w1)).reshape(chi, FOLD)
    w1_open = jnp.where(same, jnp.concatenate([w1_all] * (chi // FOLD), axis=1), 0.0)
    w1_fold = w1_open[:WIDE] + w1_open[WIDE:]
    w2 = next_w(jnp.dot(enl, w1_fold, preferred_element_type=F32))

    new_part = jnp.dot(near, part_bf, preferred_element_type=F32)
    new_part = fold_lanes(jnp.where(same, new_part, 0.0), FOLD).astype(BF16)
    last = exchange(
        jnp.concatenate([spread(w2), new_part.reshape(chips, pair_rows, FOLD)], axis=2)
    )
    w2_all = last[:, :, :FOLD].reshape(chi, FOLD)
    new_sum = jnp.sum(last[:, :, FOLD:].astype(F32), axis=0)
    new_own = pick(new_sum[:rows], new_sum[rows:])
    new_other = swap_cores(pick(new_sum[rows:], new_sum[:rows]))

    def open_new(x):
        return jnp.where(row_mask, jnp.concatenate([x] * (chi // FOLD), axis=1), 0.0).astype(BF16)

    new_left = open_new(pick(new_own, new_other))
    new_right = open_new(pick(new_other, new_own))

    w2_open = jnp.where(same, jnp.concatenate([w2_all] * (chi // FOLD), axis=1), 0.0)
    mid = jnp.dot(w2_open, near, preferred_element_type=F32).astype(BF16)
    mid_other = swap_cores(mid)
    grad_left = contract_last(edge_flat, pick(mid, mid_other)).astype(BF16)
    grad_right = contract_last(edge_flat, pick(mid_other, mid)).astype(BF16)
    return (
        new_left[None],
        new_right[None],
        grad_left.reshape(1, rows, depth, chi),
        grad_right.reshape(1, rows, depth, chi),
    )


def solution(mesh):
    row = P("site", "blk", None)
    flat = P("site", "blk", None, None)
    return jax.shard_map(
        body,
        mesh=mesh,
        in_specs=(row, flat, flat, flat, P("site", None), row, row),
        out_specs=(row, row, flat, flat),
        check_vma=False,
    )
```

```python
import jax
import jax.numpy as jnp
from jax import lax
from jax.experimental import pallas as pl
from jax.experimental.pallas import tpu as pltpu
from jax.sharding import PartitionSpec as P

SECTORS = 16
FOLD = 128
WIDE = 384
F32 = jnp.float32
BF16 = jnp.bfloat16
VMEM = pl.BlockSpec(memory_space=pltpu.VMEM)
ANY = pl.BlockSpec(memory_space=pl.ANY)


def contract_first(left, right):
    return lax.dot_general(left, right, (((0,), (0,)), ((), ())), preferred_element_type=F32)


def contract_last(left, right):
    return lax.dot_general(left, right, (((1,), (1,)), ((), ())), preferred_element_type=F32)


def fold_lanes(x, width):
    pieces = [x[:, at : at + width] for at in range(0, x.shape[1], width)]
    total = pieces[0]
    for piece in pieces[1:]:
        total = total + piece
    return total


def near_tiles(i, tiles):
    return max(0, i - 1), min(tiles, i + 2)


def sum_kernel(got_ref, out_ref):
    total = got_ref[0, :, :WIDE].astype(F32)
    for q in range(1, got_ref.shape[0]):
        total = total + got_ref[q, :, :WIDE].astype(F32)
    out_ref[...] = jnp.broadcast_to(total.astype(BF16)[None], out_ref.shape)


def fold_back(enl_ref, operand, contract, to_row_ref, to_col_ref, out_ref):
    tiles = out_ref.shape[0] // FOLD
    for i in range(tiles):
        low, high = near_tiles(i, tiles)
        rows = slice(FOLD * i, FOLD * (i + 1))
        back = contract(enl_ref[rows, :], operand(FOLD * low, FOLD * high))
        total = jnp.zeros((FOLD, FOLD), F32)
        for q in range(low, high):
            same = to_col_ref[rows, :] == to_row_ref[:, FOLD * q : FOLD * (q + 1)]
            total = total + jnp.where(same, back[:, FOLD * (q - low) : FOLD * (q - low + 1)], 0.0)
        out_ref[rows, :] = total.astype(out_ref.dtype)


def first_kernel(w_ref, enl_ref, row_ref, col_ref, to_row_ref, to_col_ref, out_ref, open_ref):
    w = w_ref[...].astype(F32)
    for q in range(WIDE // FOLD):
        same = col_ref[...] == row_ref[:, FOLD * q : FOLD * (q + 1)]
        again = col_ref[...] == row_ref[:, WIDE + FOLD * q : WIDE + FOLD * (q + 1)]
        open_ref[:, FOLD * q : FOLD * (q + 1)] = jnp.where(same | again, w, 0.0).astype(BF16)
    fold_back(
        enl_ref, lambda at, to: open_ref[at:to, :], contract_last, to_row_ref, to_col_ref, out_ref
    )


def second_kernel(cot_ref, back_ref, enl_ref, row_ref, col_ref, to_row_ref, to_col_ref, out_ref, open_ref):
    w = (cot_ref[...].astype(F32) + back_ref[...].astype(F32)).astype(BF16).astype(F32)
    for q in range(out_ref.shape[0] // FOLD):
        lanes = slice(FOLD * q, FOLD * (q + 1))
        total = jnp.where(col_ref[:WIDE, :] == row_ref[:, lanes], w[:WIDE], 0.0)
        total = total + jnp.where(col_ref[WIDE:, :] == row_ref[:, lanes], w[WIDE:], 0.0)
        open_ref[:, lanes] = total.astype(BF16)

    def product(left, right):
        return jnp.dot(left, right, preferred_element_type=F32)

    fold_back(
        enl_ref, lambda at, to: open_ref[:, at:to], product, to_row_ref, to_col_ref, out_ref
    )


SLOTS = 4
STEP = 256


def grad_kernel(
    edge_ref, near_ref, near_other_ref, w_ref, w_other_ref, row_ref, col_ref, left_ref, right_ref,
    open_ref, mid_ref, stage_ref, sems,
):
    core = lax.rem(lax.axis_index("blk"), 2)
    chi = near_ref.shape[0]
    tiles = chi // FOLD
    steps = edge_ref.shape[0] // STEP
    for side, (near, w) in enumerate(((near_ref, w_ref), (near_other_ref, w_other_ref))):
        for i in range(tiles):
            low, high = near_tiles(i, tiles)
            rows = slice(FOLD * i, FOLD * (i + 1))
            x = w[rows, :].astype(F32)
            for q in range(low, high):
                same = col_ref[rows, :] == row_ref[:, FOLD * q : FOLD * (q + 1)]
                open_ref[:, FOLD * (q - low) : FOLD * (q - low + 1)] = jnp.where(same, x, 0.0).astype(BF16)
            mid_ref[rows, :] = jnp.dot(
                open_ref[:, : FOLD * (high - low)],
                near[FOLD * low : FOLD * high, :],
                preferred_element_type=F32,
            ).astype(BF16)
        for n in range(steps):
            at = side * steps + n
            slot = at % SLOTS
            rows = pl.ds(STEP * n, STEP)
            if at >= SLOTS:
                pltpu.make_async_copy(stage_ref.at[slot], left_ref.at[rows], sems.at[slot]).wait()
            stage_ref[slot] = contract_last(edge_ref[STEP * n : STEP * (n + 1), :], mid_ref[...]).astype(BF16)

            @pl.when(core == side)
            def _():
                pltpu.make_async_copy(stage_ref.at[slot], left_ref.at[rows], sems.at[slot]).start()

            @pl.when(core != side)
            def _():
                pltpu.make_async_copy(stage_ref.at[slot], right_ref.at[rows], sems.at[slot]).start()

    for slot in range(SLOTS):
        pltpu.make_async_copy(stage_ref.at[slot], left_ref.at[pl.ds(0, STEP)], sems.at[slot]).wait()


def call(kernel, out_shape, in_specs, scratch, name, flops, moved, out_specs=VMEM):
    return pl.pallas_call(
        kernel,
        out_shape=out_shape,
        in_specs=in_specs,
        out_specs=out_specs,
        scratch_shapes=scratch,
        name=name,
        cost_estimate=pl.CostEstimate(flops=flops, bytes_accessed=moved, transcendentals=0),
        compiler_params=pltpu.CompilerParams(vmem_limit_bytes=24 << 20),
    )


def body(corner, edge, proj_left, proj_right, charge, cot_left, cot_right):
    sites = lax.axis_size("site")
    members = lax.axis_size("blk")
    rows, chi = corner.shape[1], corner.shape[2]
    depth = edge.shape[2]
    chips = members // 2
    pair_rows = 2 * rows
    blk = lax.axis_index("blk")
    first = blk % 2 == 0
    groups = [[2 * q + core for q in range(chips)] for core in range(2)]

    def swap_cores(x):
        return lax.ppermute(x, "blk", [(i, i ^ 1) for i in range(members)])

    def site_move(x, distance, cross):
        route = []
        for s in range(sites):
            for i in range(members):
                target = i ^ 1 if cross else i
                sign = 1 if target % 2 == 0 else -1
                route.append((s * members + i, ((s + sign * distance) % sites) * members + target))
        return lax.ppermute(x, ("site", "blk"), route)

    def exchange(x):
        return lax.all_to_all(x, "blk", 0, 0, tiled=True, axis_index_groups=groups)

    def spread(x):
        return jnp.broadcast_to(x[None], (chips,) + x.shape)

    def pick(a, b):
        return jnp.where(first, a, b)

    def weave(own, other):
        halves = jnp.stack([pick(own, other), pick(other, own)], axis=1)
        return halves.reshape(chi, own.shape[-1])

    row_label_all = charge
    label = charge[0]
    to_row = site_move(charge, 1, False)
    label_to = to_row[0]
    col = label[:, None]
    to_col = label_to[:, None]
    row_label = lax.dynamic_slice_in_dim(label, blk * rows, rows, 0)
    row_mask = row_label[:, None] == label[None, :]
    here = corner[0]
    start_left = fold_lanes(jnp.where(row_mask, cot_left[0], 0.0), FOLD).astype(BF16)
    start_right = fold_lanes(jnp.where(row_mask, cot_right[0], 0.0), FOLD).astype(BF16)
    tall = jnp.concatenate([here[:, :WIDE], here[:, WIDE:]], axis=0)
    start = jnp.concatenate([tall, jnp.concatenate([start_left, start_right], axis=0)], axis=1)

    edge_flat = edge[0].reshape(rows * depth, chi)
    part_left = contract_first(edge_flat, proj_left[0].reshape(rows * depth, chi))
    part_right = contract_first(edge_flat, proj_right[0].reshape(rows * depth, chi))
    other_part = swap_cores(pick(part_right, part_left).astype(BF16))
    part = pick(part_left, part_right) + other_part.astype(F32)
    part_bf = part.astype(BF16)

    sector = jnp.arange(SECTORS, dtype=jnp.int32)
    in_sector = label_to[None, :] == sector[:, None]
    least = jnp.min(jnp.where(in_sector, label[None, :], SECTORS), axis=1)
    most = jnp.max(jnp.where(in_sector, label[None, :], -1), axis=1)
    low = jnp.sum(jnp.where(label_to[:, None] == sector[None, :], least[None, :], 0), axis=1)
    high = jnp.sum(jnp.where(label_to[:, None] == sector[None, :], most[None, :], 0), axis=1)
    reach = (label[None, :] >= low[:, None]) & (label[None, :] <= high[:, None])
    narrow = fold_lanes(jnp.where(reach, part, 0.0), WIDE).astype(BF16)
    got = exchange(jnp.concatenate([narrow.reshape(chips, pair_rows, WIDE), spread(start)], axis=2))

    summed = call(
        sum_kernel, jax.ShapeDtypeStruct((chips, pair_rows, WIDE), BF16), [VMEM], [], "sum_enl", 0, 2 << 20
    )(got)
    enl = exchange(summed).reshape(chi, WIDE)

    half = jnp.concatenate([got[:, :rows, WIDE : 2 * WIDE], got[:, rows:, WIDE : 2 * WIDE]], axis=2)
    near = weave(site_move(half, 1, False), site_move(half, 1, True))
    near_other = swap_cores(near)
    early_left = got[:, :rows, 2 * WIDE :]
    early_right = got[:, rows:, 2 * WIDE :]
    w0 = weave(pick(early_left, early_right), swap_cores(pick(early_right, early_left)))

    same = label[:, None] == label[None, :]
    w0_open = jnp.where(same, jnp.concatenate([w0] * (chi // FOLD), axis=1), 0.0)
    cot = jnp.transpose(jnp.sum(w0_open.reshape(chi // FOLD, FOLD, chi), axis=0))

    packed = jax.ShapeDtypeStruct((chi, FOLD), BF16)
    back1 = call(
        first_kernel, packed, [VMEM] * 6, [pltpu.VMEM((chi, WIDE), BF16)], "first_back", chi * chi * WIDE, 2 << 20
    )(w0, enl, row_label_all, col, to_row, to_col)
    back1_at = site_move(back1, -1, False)

    near_part, back1_tie = lax.optimization_barrier((part_bf, back1))
    new_part = jnp.dot(near, near_part, preferred_element_type=F32)
    new_part = fold_lanes(jnp.where(same, new_part, 0.0), FOLD).astype(BF16)
    new_got = exchange(new_part.reshape(chips, pair_rows, FOLD))

    back2 = call(
        second_kernel, packed, [VMEM] * 7, [pltpu.VMEM((WIDE, chi), BF16)], "second_back", chi * chi * WIDE, 2 << 20
    )(cot, back1_at, enl, row_label_all, col, to_row, to_col)
    w2 = (cot.astype(F32) + site_move(back2, -1, False).astype(F32)).astype(BF16)
    w2_other = swap_cores(w2)

    new_sum = jnp.sum(new_got.astype(F32), axis=0)
    new_own = pick(new_sum[:rows], new_sum[rows:])
    new_other = swap_cores(pick(new_sum[rows:], new_sum[:rows]))

    def open_new(x):
        return jnp.where(row_mask, jnp.concatenate([x] * (chi // FOLD), axis=1), 0.0).astype(BF16)

    new_left = open_new(pick(new_own, new_other))
    new_right = open_new(pick(new_other, new_own))

    flat = jax.ShapeDtypeStruct((rows * depth, chi), BF16)
    grad_left, grad_right = call(
        grad_kernel,
        (flat, flat),
        [VMEM] * 7,
        [
            pltpu.VMEM((FOLD, WIDE), BF16),
            pltpu.VMEM((chi, chi), BF16),
            pltpu.VMEM((SLOTS, STEP, chi), BF16),
            pltpu.SemaphoreType.DMA((SLOTS,)),
        ],
        "grads",
        4 * rows * depth * chi * chi,
        8 << 20,
        (ANY, ANY),
    )(edge_flat, near, near_other, w2, w2_other, row_label_all, col)
    return (
        new_left[None],
        new_right[None],
        grad_left.reshape(1, rows, depth, chi),
        grad_right.reshape(1, rows, depth, chi),
    )


def solution(mesh):
    row = P("site", "blk", None)
    flat = P("site", "blk", None, None)
    return jax.shard_map(
        body,
        mesh=mesh,
        in_specs=(row, flat, flat, flat, P("site", None), row, row),
        out_specs=(row, row, flat, flat),
        check_vma=False,
    )
```

```python
import jax
import jax.numpy as jnp
from jax import lax
from jax.experimental import pallas as pl
from jax.experimental.pallas import tpu as pltpu
from jax.sharding import PartitionSpec as P


SECTORS = 16
FOLD = 128
WIDE = 384
F32 = jnp.float32
BF16 = jnp.bfloat16
VMEM = pl.BlockSpec(memory_space=pltpu.VMEM)
ANY = pl.BlockSpec(memory_space=pl.ANY)


def contract_first(left, right):
    return lax.dot_general(left, right, (((0,), (0,)), ((), ())), preferred_element_type=F32)


def contract_last(left, right):
    return lax.dot_general(left, right, (((1,), (1,)), ((), ())), preferred_element_type=F32)


def fold_lanes(x, width):
    pieces = [x[:, at : at + width] for at in range(0, x.shape[1], width)]
    total = pieces[0]
    for piece in pieces[1:]:
        total = total + piece
    return total


def near_tiles(i, tiles):
    return max(0, i - 1), min(tiles, i + 2)


def pack_kernel(
    part_ref, other_ref, low_ref, high_ref, row_ref, corner_ref, cot_left_ref, cot_right_ref, own_ref,
    out_ref, part_out_ref,
):
    chips, pair_rows = out_ref.shape[:2]
    rows = pair_rows // 2
    for q in range(chips):
        at = slice(pair_rows * q, pair_rows * (q + 1))
        part = part_ref[at, :] + other_ref[at, :].astype(F32)
        part_out_ref[at, :] = part.astype(BF16)
        label = row_ref[...]
        part = jnp.where((label >= low_ref[at, :]) & (label <= high_ref[at, :]), part, 0.0)
        out_ref[q, :, :WIDE] = (part[:, :WIDE] + part[:, WIDE:]).astype(BF16)
    mask = own_ref[...] == row_ref[...]
    for q in range(chips):
        out_ref[q, :rows, WIDE : 2 * WIDE] = corner_ref[:, :WIDE]
        out_ref[q, rows:, WIDE : 2 * WIDE] = corner_ref[:, WIDE:]
    for n, cot_ref in enumerate((cot_left_ref, cot_right_ref)):
        cot = fold_lanes(jnp.where(mask, cot_ref[...], 0.0), FOLD).astype(BF16)
        for q in range(chips):
            out_ref[q, rows * n : rows * (n + 1), 2 * WIDE :] = cot


def sum_kernel(got_ref, out_ref, corner_ref, early_ref):
    total = got_ref[0, :, :WIDE].astype(F32)
    for q in range(1, got_ref.shape[0]):
        total = total + got_ref[q, :, :WIDE].astype(F32)
    out_ref[...] = jnp.broadcast_to(total.astype(BF16)[None], out_ref.shape)
    corner_ref[...] = got_ref[:, :, WIDE : 2 * WIDE]
    early_ref[...] = got_ref[:, :, 2 * WIDE :]


def start_kernel(early_ref, other_ref, row_ref, col_ref, w_ref, cot_ref):
    chips, pair_rows, _ = early_ref.shape
    rows = pair_rows // 2
    core = lax.rem(lax.axis_index("blk"), 2)

    @pl.when(core == 0)
    def _():
        for q in range(chips):
            w_ref[pair_rows * q : pair_rows * q + rows, :] = early_ref[q, :rows, :]
            w_ref[pair_rows * q + rows : pair_rows * (q + 1), :] = other_ref[q, :rows, :]

    @pl.when(core == 1)
    def _():
        for q in range(chips):
            w_ref[pair_rows * q : pair_rows * q + rows, :] = other_ref[q, rows:, :]
            w_ref[pair_rows * q + rows : pair_rows * (q + 1), :] = early_ref[q, rows:, :]

    tiles = w_ref.shape[0] // FOLD
    for i in range(tiles):
        low, high = near_tiles(i, tiles)
        lanes = slice(FOLD * i, FOLD * (i + 1))
        total = jnp.zeros((FOLD, FOLD), F32)
        for q in range(low, high):
            at = slice(FOLD * q, FOLD * (q + 1))
            same = col_ref[at, :] == row_ref[:, lanes]
            total = total + jnp.where(same, w_ref[at, :].astype(F32), 0.0)
        cot_ref[lanes, :] = total.T


def weave_kernel(same_ref, cross_ref, out_ref):
    chips, pair_rows, width = same_ref.shape
    rows = pair_rows // 2
    core = lax.rem(lax.axis_index("blk"), 2)

    def put(low_ref, high_ref):
        for q in range(chips):
            for n, ref in enumerate((low_ref, high_ref)):
                at = pair_rows * q + rows * n
                out_ref[at : at + rows, :width] = ref[q, :rows, :]
                out_ref[at : at + rows, width:] = ref[q, rows:, :]

    @pl.when(core == 0)
    def _():
        put(same_ref, cross_ref)

    @pl.when(core == 1)
    def _():
        put(cross_ref, same_ref)


def new_kernel(near_ref, part_ref, row_ref, col_ref, out_ref):
    tiles = near_ref.shape[0] // FOLD
    for i in range(tiles):
        low, high = near_tiles(i, tiles)
        rows = slice(FOLD * i, FOLD * (i + 1))
        product = jnp.dot(
            near_ref[rows, :], part_ref[:, FOLD * low : FOLD * high], preferred_element_type=F32
        )
        total = jnp.zeros((FOLD, FOLD), F32)
        for q in range(low, high):
            same = col_ref[rows, :] == row_ref[:, FOLD * q : FOLD * (q + 1)]
            total = total + jnp.where(same, product[:, FOLD * (q - low) : FOLD * (q - low + 1)], 0.0)
        out_ref[rows, :] = total.astype(BF16)


def total_kernel(got_ref, out_ref):
    total = got_ref[0].astype(F32)
    for q in range(1, got_ref.shape[0]):
        total = total + got_ref[q].astype(F32)
    out_ref[...] = total


def open_kernel(own_ref, other_ref, label_ref, row_ref, left_ref, right_ref):
    rows, chi = left_ref.shape
    core = lax.rem(lax.axis_index("blk"), 2)
    mask = label_ref[...] == row_ref[...]

    def put(out_ref, x):
        for q in range(chi // FOLD):
            lanes = slice(FOLD * q, FOLD * (q + 1))
            out_ref[:, lanes] = jnp.where(mask[:, lanes], x, 0.0).astype(BF16)

    @pl.when(core == 0)
    def _():
        put(left_ref, own_ref[:rows, :])
        put(right_ref, other_ref[:rows, :])

    @pl.when(core == 1)
    def _():
        put(right_ref, own_ref[rows:, :])
        put(left_ref, other_ref[rows:, :])


def fold_back(enl_ref, operand, contract, to_row_ref, to_col_ref, out_ref):
    tiles = out_ref.shape[0] // FOLD
    for i in range(tiles):
        low, high = near_tiles(i, tiles)
        rows = slice(FOLD * i, FOLD * (i + 1))
        back = contract(enl_ref[rows, :], operand(FOLD * low, FOLD * high))
        total = jnp.zeros((FOLD, FOLD), F32)
        for q in range(low, high):
            same = to_col_ref[rows, :] == to_row_ref[:, FOLD * q : FOLD * (q + 1)]
            total = total + jnp.where(same, back[:, FOLD * (q - low) : FOLD * (q - low + 1)], 0.0)
        out_ref[rows, :] = total.astype(out_ref.dtype)


def first_kernel(w_ref, enl_ref, row_ref, col_ref, to_row_ref, to_col_ref, out_ref, open_ref):
    w = w_ref[...].astype(F32)
    for q in range(WIDE // FOLD):
        same = col_ref[...] == row_ref[:, FOLD * q : FOLD * (q + 1)]
        again = col_ref[...] == row_ref[:, WIDE + FOLD * q : WIDE + FOLD * (q + 1)]
        open_ref[:, FOLD * q : FOLD * (q + 1)] = jnp.where(same | again, w, 0.0).astype(BF16)
    fold_back(
        enl_ref, lambda at, to: open_ref[at:to, :], contract_last, to_row_ref, to_col_ref, out_ref
    )


def second_kernel(cot_ref, back_ref, enl_ref, row_ref, col_ref, to_row_ref, to_col_ref, out_ref, open_ref):
    w = (cot_ref[...].astype(F32) + back_ref[...].astype(F32)).astype(BF16).astype(F32)
    for q in range(out_ref.shape[0] // FOLD):
        lanes = slice(FOLD * q, FOLD * (q + 1))
        total = jnp.where(col_ref[:WIDE, :] == row_ref[:, lanes], w[:WIDE], 0.0)
        total = total + jnp.where(col_ref[WIDE:, :] == row_ref[:, lanes], w[WIDE:], 0.0)
        open_ref[:, lanes] = total.astype(BF16)

    def product(left, right):
        return jnp.dot(left, right, preferred_element_type=F32)

    fold_back(
        enl_ref, lambda at, to: open_ref[:, at:to], product, to_row_ref, to_col_ref, out_ref
    )


SLOTS = 4
STEP = 256


def grad_kernel(
    edge_ref, near_ref, near_other_ref, w_ref, w_other_ref, row_ref, col_ref, left_ref, right_ref,
    open_ref, mid_ref, stage_ref, sems,
):
    core = lax.rem(lax.axis_index("blk"), 2)
    chi = near_ref.shape[0]
    tiles = chi // FOLD
    steps = edge_ref.shape[0] // STEP
    for side, (near, w) in enumerate(((near_ref, w_ref), (near_other_ref, w_other_ref))):
        for i in range(tiles):
            low, high = near_tiles(i, tiles)
            rows = slice(FOLD * i, FOLD * (i + 1))
            x = w[rows, :].astype(F32)
            for q in range(low, high):
                same = col_ref[rows, :] == row_ref[:, FOLD * q : FOLD * (q + 1)]
                open_ref[:, FOLD * (q - low) : FOLD * (q - low + 1)] = jnp.where(same, x, 0.0).astype(BF16)
            mid_ref[rows, :] = jnp.dot(
                open_ref[:, : FOLD * (high - low)],
                near[FOLD * low : FOLD * high, :],
                preferred_element_type=F32,
            ).astype(BF16)
        for n in range(steps):
            at = side * steps + n
            slot = at % SLOTS
            rows = pl.ds(STEP * n, STEP)
            if at >= SLOTS:
                pltpu.make_async_copy(stage_ref.at[slot], left_ref.at[rows], sems.at[slot]).wait()
            stage_ref[slot] = contract_last(edge_ref[STEP * n : STEP * (n + 1), :], mid_ref[...]).astype(BF16)

            @pl.when(core == side)
            def _():
                pltpu.make_async_copy(stage_ref.at[slot], left_ref.at[rows], sems.at[slot]).start()

            @pl.when(core != side)
            def _():
                pltpu.make_async_copy(stage_ref.at[slot], right_ref.at[rows], sems.at[slot]).start()

    for slot in range(SLOTS):
        pltpu.make_async_copy(stage_ref.at[slot], left_ref.at[pl.ds(0, STEP)], sems.at[slot]).wait()


def call(kernel, out_shape, in_specs, scratch, flops, moved, out_specs=VMEM):
    return pl.pallas_call(
        kernel,
        out_shape=out_shape,
        in_specs=in_specs,
        out_specs=out_specs,
        scratch_shapes=scratch,
        cost_estimate=pl.CostEstimate(flops=flops, bytes_accessed=moved, transcendentals=0),
        compiler_params=pltpu.CompilerParams(vmem_limit_bytes=24 << 20),
    )


def body(corner, edge, proj_left, proj_right, charge, cot_left, cot_right):
    sites = lax.axis_size("site")
    members = lax.axis_size("blk")
    rows, chi = corner.shape[1], corner.shape[2]
    depth = edge.shape[2]
    chips = members // 2
    pair_rows = 2 * rows
    blk = lax.axis_index("blk")
    first = blk % 2 == 0
    groups = [[2 * q + core for q in range(chips)] for core in range(2)]

    def swap_cores(x):
        return lax.ppermute(x, "blk", [(i, i ^ 1) for i in range(members)])

    def site_move(x, distance, cross):
        route = []
        for s in range(sites):
            for i in range(members):
                target = i ^ 1 if cross else i
                sign = 1 if target % 2 == 0 else -1
                route.append((s * members + i, ((s + sign * distance) % sites) * members + target))
        return lax.ppermute(x, ("site", "blk"), route)

    def exchange(x):
        return lax.all_to_all(x, "blk", 0, 0, tiled=True, axis_index_groups=groups)

    def pick(a, b):
        return jnp.where(first, a, b)

    row = charge
    label = charge[0]
    to_row = site_move(charge, 1, False)
    label_to = to_row[0]
    col = label[:, None]
    to_col = label_to[:, None]
    own_label = lax.dynamic_slice_in_dim(label, blk * rows, rows, 0)[:, None]

    edge_flat = edge[0].reshape(rows * depth, chi)
    part_left = contract_first(edge_flat, proj_left[0].reshape(rows * depth, chi))
    part_right = contract_first(edge_flat, proj_right[0].reshape(rows * depth, chi))
    other_part = swap_cores(pick(part_right, part_left).astype(BF16))
    part = pick(part_left, part_right)

    sector = jnp.arange(SECTORS, dtype=jnp.int32)
    in_sector = label_to[None, :] == sector[:, None]
    least = jnp.min(jnp.where(in_sector, label[None, :], SECTORS), axis=1)
    most = jnp.max(jnp.where(in_sector, label[None, :], -1), axis=1)
    low = jnp.sum(jnp.where(label_to[:, None] == sector[None, :], least[None, :], 0), axis=1)
    high = jnp.sum(jnp.where(label_to[:, None] == sector[None, :], most[None, :], 0), axis=1)

    def array(*shape, dtype=BF16):
        return jax.ShapeDtypeStruct(shape, dtype)

    packed, part_bf = call(
        pack_kernel,
        (array(chips, pair_rows, 2 * WIDE + FOLD), array(chi, chi)),
        [VMEM] * 9,
        [],
        chi * chi * 8,
        6 << 20,
        (VMEM, VMEM),
    )(part, other_part, low[:, None], high[:, None], row, corner[0], cot_left[0], cot_right[0], own_label)
    got = exchange(packed)
    summed, corner_half, early = call(
        sum_kernel,
        (array(chips, pair_rows, WIDE), array(chips, pair_rows, WIDE), array(chips, pair_rows, FOLD)),
        [VMEM],
        [],
        0,
        3 << 20,
        (VMEM, VMEM, VMEM),
    )(got)
    enl = exchange(summed).reshape(chi, WIDE)

    early_other = swap_cores(early)
    w0, cot = call(
        start_kernel, (array(chi, FOLD), array(chi, FOLD, dtype=F32)), [VMEM] * 4, [], 0, 1 << 20, (VMEM, VMEM)
    )(early, early_other, row, col)
    corner_same = site_move(corner_half, 1, False)
    corner_cross = site_move(corner_half, 1, True)
    near = call(weave_kernel, array(chi, chi), [VMEM] * 2, [], 0, 3 << 20)(corner_same, corner_cross)
    near_other = swap_cores(near)

    back1 = call(
        first_kernel, array(chi, FOLD), [VMEM] * 6, [pltpu.VMEM((chi, WIDE), BF16)], chi * chi * WIDE, 2 << 20
    )(w0, enl, row, col, to_row, to_col)
    back1_at = site_move(back1, -1, False)
    back2 = call(
        second_kernel, array(chi, FOLD), [VMEM] * 7, [pltpu.VMEM((WIDE, chi), BF16)], chi * chi * WIDE, 2 << 20
    )(cot, back1_at, enl, row, col, to_row, to_col)
    back2_at = site_move(back2, -1, False)
    w2 = (cot + back2_at.astype(F32)).astype(BF16)
    w2_other = swap_cores(w2)

    new_part = call(new_kernel, array(chi, FOLD), [VMEM] * 4, [], chi * chi * chi, 3 << 20)(near, part_bf, row, col)
    new_got = exchange(new_part.reshape(chips, pair_rows, FOLD))
    new_sum = call(total_kernel, array(pair_rows, FOLD, dtype=F32), [VMEM], [], 0, 1 << 18)(new_got)
    new_other = swap_cores(new_sum)
    new_left, new_right = call(
        open_kernel, (array(rows, chi), array(rows, chi)), [VMEM] * 4, [], 0, 1 << 17, (VMEM, VMEM)
    )(new_sum, new_other, own_label, row)

    flat = array(rows * depth, chi)
    grad_left, grad_right = call(
        grad_kernel,
        (flat, flat),
        [VMEM] * 7,
        [
            pltpu.VMEM((FOLD, WIDE), BF16),
            pltpu.VMEM((chi, chi), BF16),
            pltpu.VMEM((SLOTS, STEP, chi), BF16),
            pltpu.SemaphoreType.DMA((SLOTS,)),
        ],
        4 * rows * depth * chi * chi,
        8 << 20,
        (ANY, ANY),
    )(edge_flat, near, near_other, w2, w2_other, row, col)
    return (
        new_left[None],
        new_right[None],
        grad_left.reshape(1, rows, depth, chi),
        grad_right.reshape(1, rows, depth, chi),
    )


def solution(mesh):
    row = P("site", "blk", None)
    flat = P("site", "blk", None, None)

    return jax.shard_map(
        body,
        mesh=mesh,
        in_specs=(row, flat, flat, flat, P("site", None), row, row),
        out_specs=(row, row, flat, flat),
        check_vma=False,
    )
```

```python
import jax
import jax.numpy as jnp
from jax import lax
from jax.experimental import pallas as pl
from jax.experimental.pallas import tpu as pltpu
from jax.sharding import PartitionSpec as P


SECTORS = 16
FOLD = 128
WIDE = 384
F32 = jnp.float32
BF16 = jnp.bfloat16
VMEM = pl.BlockSpec(memory_space=pltpu.VMEM)
ANY = pl.BlockSpec(memory_space=pl.ANY)
HBM = pl.BlockSpec(memory_space=pltpu.HBM)


def contract_first(left, right):
    return lax.dot_general(left, right, (((0,), (0,)), ((), ())), preferred_element_type=F32)


def contract_last(left, right):
    return lax.dot_general(left, right, (((1,), (1,)), ((), ())), preferred_element_type=F32)


def fold_lanes(x, width):
    pieces = [x[:, at : at + width] for at in range(0, x.shape[1], width)]
    total = pieces[0]
    for piece in pieces[1:]:
        total = total + piece
    return total


def near_tiles(i, tiles):
    return max(0, i - 1), min(tiles, i + 2)


def label_row(ref):
    return ref[...].astype(F32)


def column(row, i):
    return jnp.broadcast_to(row[:, FOLD * i : FOLD * (i + 1)], (FOLD, FOLD)).T


def lanes(q):
    return slice(FOLD * q, FOLD * (q + 1))


def pack_kernel(
    left_ref, right_ref, other_ref, row_ref, to_row_ref, cot_left_ref, cot_right_ref,
    out_ref, stage_ref, cot_ref, sems,
):
    chi = left_ref.shape[0]
    rows = cot_ref.shape[1]
    tiles = chi // FOLD
    wide = WIDE // FOLD
    blk = lax.axis_index("blk")
    copies = [
        pltpu.make_async_copy(ref, cot_ref.at[n], sems.at[n])
        for n, ref in enumerate((cot_left_ref, cot_right_ref))
    ]
    for copy in copies:
        copy.start()
    row, to_row = label_row(row_ref), label_row(to_row_ref)
    low, high = jnp.zeros_like(row), jnp.zeros_like(row)
    for n in range(SECTORS):
        member = to_row == float(n)
        least = jnp.min(jnp.where(member, row, float(SECTORS)), axis=1, keepdims=True)
        most = jnp.max(jnp.where(member, row, -1.0), axis=1, keepdims=True)
        low = low + jnp.where(member, least, 0.0)
        high = high + jnp.where(member, most, 0.0)

    def fold(own_ref):
        for i in range(tiles):
            at = lanes(i)
            low_col, high_col = column(low, i), column(high, i)
            totals = [None] * wide
            for q in range(tiles):
                part = own_ref[at, lanes(q)] + other_ref[at, lanes(q)].astype(F32)
                label = row[:, lanes(q)]
                part = jnp.where((label >= low_col) & (label <= high_col), part, 0.0)
                old = totals[q % wide]
                totals[q % wide] = part if old is None else old + part
            for q in range(wide):
                stage_ref[at, lanes(q)] = totals[q].astype(BF16)

    @pl.when(lax.rem(blk, 2) == 0)
    def _():
        fold(left_ref)

    @pl.when(lax.rem(blk, 2) == 1)
    def _():
        fold(right_ref)

    position = lax.broadcasted_iota(jnp.int32, (rows, chi), 1)
    wanted = blk * rows + lax.broadcasted_iota(jnp.int32, (rows, chi), 0)
    own = jnp.sum(jnp.where(position == wanted, row, 0.0), axis=1, keepdims=True)
    mask = own == row
    for n, copy in enumerate(copies):
        copy.wait()
        cot = fold_lanes(jnp.where(mask, cot_ref[n], 0.0), FOLD).astype(BF16)
        for q in range(chi // (2 * rows)):
            at = 2 * rows * q + rows * n
            stage_ref[at : at + rows, WIDE:] = cot
    copy = pltpu.make_async_copy(stage_ref, out_ref, sems.at[2])
    copy.start()
    copy.wait()


def sum_kernel(got_ref, out_ref, early_ref, held_ref, total_ref, sems):
    chips = got_ref.shape[0]
    part = chips // 4
    copies = [
        pltpu.make_async_copy(
            got_ref.at[pl.ds(part * n, part)], held_ref.at[pl.ds(part * n, part)], sems.at[n]
        )
        for n in range(4)
    ]
    for copy in copies:
        copy.start()
    total = jnp.zeros(total_ref.shape, F32)
    for n, copy in enumerate(copies):
        copy.wait()
        for q in range(part * n, part * (n + 1)):
            total = total + held_ref[q, :, :WIDE].astype(F32)
    total_ref[...] = total.astype(BF16)
    for q in range(chips):
        pltpu.make_async_copy(total_ref, out_ref.at[q], sems.at[q]).start()
    early_ref[...] = held_ref[:, :, WIDE:]
    for q in range(chips):
        pltpu.make_async_copy(total_ref, out_ref.at[q], sems.at[q]).wait()


def start_kernel(early_ref, other_ref, row_ref, open_ref, cot_ref, w_ref):
    chips, pair_rows, _ = early_ref.shape
    rows = pair_rows // 2
    core = lax.rem(lax.axis_index("blk"), 2)

    @pl.when(core == 0)
    def _():
        for q in range(chips):
            w_ref[pair_rows * q : pair_rows * q + rows, :] = early_ref[q, :rows, :]
            w_ref[pair_rows * q + rows : pair_rows * (q + 1), :] = other_ref[q, :rows, :]

    @pl.when(core == 1)
    def _():
        for q in range(chips):
            w_ref[pair_rows * q : pair_rows * q + rows, :] = other_ref[q, rows:, :]
            w_ref[pair_rows * q + rows : pair_rows * (q + 1), :] = early_ref[q, rows:, :]

    row = label_row(row_ref)
    tiles = w_ref.shape[0] // FOLD
    wide = WIDE // FOLD
    cols = [column(row, i) for i in range(tiles)]
    for i in range(tiles):
        low, high = near_tiles(i, tiles)
        total = jnp.zeros((FOLD, FOLD), F32)
        for q in range(low, high):
            total = total + jnp.where(cols[q] == row[:, lanes(i)], w_ref[lanes(q), :].astype(F32), 0.0)
        cot_ref[lanes(i), :] = total.T.astype(BF16)
        w = w_ref[lanes(i), :].astype(F32)
        for q in range(wide):
            same = (cols[i] == row[:, lanes(q)]) | (cols[i] == row[:, lanes(wide + q)])
            open_ref[lanes(i), lanes(q)] = jnp.where(same, w, 0.0).astype(BF16)


def weave_kernel(*refs):
    *piece_refs, out_ref, sems = refs
    ring = len(piece_refs)
    block = piece_refs[0].shape[0] // 2
    chip = lax.div(lax.axis_index("blk"), 2)
    y, z = lax.div(chip, ring), lax.rem(chip, ring)
    copies = []
    for n, ref in enumerate(piece_refs):
        step = -((n + 1) // 2) if n % 2 else n // 2
        for half in range(2):
            source = lax.rem(y + half, 2) * ring + lax.rem(z + step + ring, ring)
            at = pl.multiple_of(source * block, 16)
            copies.append(
                pltpu.make_async_copy(
                    ref.at[pl.ds(block * half, block)], out_ref.at[pl.ds(at, block)], sems.at[2 * n + half]
                )
            )
    for copy in copies:
        copy.start()
    for copy in copies:
        copy.wait()


def fold_tile(product, col, row, low, high):
    total = jnp.zeros((FOLD, FOLD), F32)
    for q in range(low, high):
        total = total + jnp.where(col == row[:, lanes(q)], product[:, lanes(q - low)], 0.0)
    return total.astype(BF16)


def new_kernel(near_ref, part_ref, row_ref, out_ref):
    tiles = near_ref.shape[0] // FOLD
    row = label_row(row_ref)
    for i in range(tiles):
        low, high = near_tiles(i, tiles)
        product = jnp.dot(
            near_ref[lanes(i), :], part_ref[:, FOLD * low : FOLD * high], preferred_element_type=F32
        )
        out_ref[lanes(i), :] = fold_tile(product, column(row, i), row, low, high)


def total_kernel(got_ref, out_ref):
    total = got_ref[0].astype(F32)
    for q in range(1, got_ref.shape[0]):
        total = total + got_ref[q].astype(F32)
    out_ref[...] = total


def open_kernel(own_ref, other_ref, row_ref, left_ref, right_ref):
    rows, chi = left_ref.shape
    blk = lax.axis_index("blk")
    core = lax.rem(blk, 2)
    row = label_row(row_ref)
    position = lax.broadcasted_iota(jnp.int32, (rows, chi), 1)
    wanted = blk * rows + lax.broadcasted_iota(jnp.int32, (rows, chi), 0)
    mask = jnp.sum(jnp.where(position == wanted, row, 0.0), axis=1, keepdims=True) == row

    def put(out_ref, x):
        wide = jnp.concatenate([x] * (chi // FOLD), axis=1)
        out_ref[...] = jnp.where(mask, wide, 0.0).astype(BF16)

    @pl.when(core == 0)
    def _():
        put(left_ref, own_ref[:rows, :])
        put(right_ref, other_ref[:rows, :])

    @pl.when(core == 1)
    def _():
        put(right_ref, own_ref[rows:, :])
        put(left_ref, other_ref[rows:, :])


def first_kernel(open_ref, enl_ref, to_row_ref, out_ref):
    to_row = label_row(to_row_ref)
    tiles = out_ref.shape[0] // FOLD
    for i in range(tiles):
        low, high = near_tiles(i, tiles)
        back = contract_last(enl_ref[lanes(i), :], open_ref[FOLD * low : FOLD * high, :])
        out_ref[lanes(i), :] = fold_tile(back, column(to_row, i), to_row, low, high)


def second_kernel(cot_ref, back_ref, enl_ref, row_ref, to_row_ref, out_ref, open_ref):
    row, to_row = label_row(row_ref), label_row(to_row_ref)
    tiles = out_ref.shape[0] // FOLD
    wide = WIDE // FOLD
    for i in range(wide):
        halves = []
        for at in (lanes(i), lanes(wide + i)):
            w = (cot_ref[at, :].astype(F32) + back_ref[at, :].astype(F32)).astype(BF16)
            halves.append(w.astype(F32))
        cols = column(row, i), column(row, wide + i)
        for q in range(tiles):
            total = jnp.where(cols[0] == row[:, lanes(q)], halves[0], 0.0)
            total = total + jnp.where(cols[1] == row[:, lanes(q)], halves[1], 0.0)
            open_ref[lanes(i), lanes(q)] = total.astype(BF16)
    for i in range(tiles):
        low, high = near_tiles(i, tiles)
        back = jnp.dot(
            enl_ref[lanes(i), :], open_ref[:, FOLD * low : FOLD * high], preferred_element_type=F32
        )
        out_ref[lanes(i), :] = fold_tile(back, column(to_row, i), to_row, low, high)


SLOTS = 4
STEP = 256


def grad_kernel(
    edge_hbm, near_hbm, other_hbm, w_ref, w_other_ref, row_ref, left_ref, right_ref,
    edge_ref, near_ref, open_ref, mid_ref, stage_ref, in_sems, sems,
):
    core = lax.rem(lax.axis_index("blk"), 2)
    chi = near_ref.shape[1]
    tiles = chi // FOLD
    steps = edge_ref.shape[0] // STEP
    row = label_row(row_ref)
    near_copies = [
        pltpu.make_async_copy(ref, near_ref.at[n], in_sems.at[steps + n])
        for n, ref in enumerate((near_hbm, other_hbm))
    ]
    edge_copies = [
        pltpu.make_async_copy(
            edge_hbm.at[pl.ds(STEP * n, STEP)], edge_ref.at[pl.ds(STEP * n, STEP)], in_sems.at[n]
        )
        for n in range(steps)
    ]
    near_copies[0].start()
    for copy in edge_copies:
        copy.start()
    near_copies[1].start()
    for side, w in enumerate((w_ref, w_other_ref)):
        near_copies[side].wait()
        for i in range(tiles):
            low, high = near_tiles(i, tiles)
            col = column(row, i)
            x = w[lanes(i), :].astype(F32)
            for q in range(low, high):
                open_ref[:, lanes(q - low)] = jnp.where(col == row[:, lanes(q)], x, 0.0).astype(BF16)
            mid = jnp.dot(
                open_ref[:, : FOLD * (high - low)],
                near_ref[side, FOLD * low : FOLD * high, :],
                preferred_element_type=F32,
            )
            mid_ref[:, lanes(i)] = mid.T.astype(BF16)
        for n in range(steps):
            at = side * steps + n
            slot = at % SLOTS
            rows = pl.ds(STEP * n, STEP)
            if side == 0:
                edge_copies[n].wait()
            if at >= SLOTS:
                pltpu.make_async_copy(stage_ref.at[slot], left_ref.at[rows], sems.at[slot]).wait()
            stage_ref[slot] = jnp.dot(
                edge_ref[STEP * n : STEP * (n + 1), :], mid_ref[...], preferred_element_type=F32
            ).astype(BF16)

            @pl.when(core == side)
            def _():
                pltpu.make_async_copy(stage_ref.at[slot], left_ref.at[rows], sems.at[slot]).start()

            @pl.when(core != side)
            def _():
                pltpu.make_async_copy(stage_ref.at[slot], right_ref.at[rows], sems.at[slot]).start()

    for slot in range(SLOTS):
        pltpu.make_async_copy(stage_ref.at[slot], left_ref.at[pl.ds(0, STEP)], sems.at[slot]).wait()


def call(kernel, out_shape, in_specs, scratch, flops, moved, out_specs=VMEM, limit=24 << 20):
    return pl.pallas_call(
        kernel,
        out_shape=out_shape,
        in_specs=in_specs,
        out_specs=out_specs,
        scratch_shapes=scratch,
        cost_estimate=pl.CostEstimate(flops=flops, bytes_accessed=moved, transcendentals=0),
        compiler_params=pltpu.CompilerParams(vmem_limit_bytes=limit),
    )


def body(corner, edge, proj_left, proj_right, charge, cot_left, cot_right):
    sites = lax.axis_size("site")
    members = lax.axis_size("blk")
    rows, chi = corner.shape[1], corner.shape[2]
    depth = edge.shape[2]
    chips = members // 2
    pair_rows = 2 * rows
    blk = lax.axis_index("blk")
    first = blk % 2 == 0
    groups = [[2 * q + core for q in range(chips)] for core in range(2)]

    def swap_cores(x):
        return lax.ppermute(x, "blk", [(i, i ^ 1) for i in range(members)])

    def site_move(x, distance, cross):
        route = []
        for s in range(sites):
            for i in range(members):
                target = i ^ 1 if cross else i
                sign = 1 if target % 2 == 0 else -1
                route.append((s * members + i, ((s + sign * distance) % sites) * members + target))
        return lax.ppermute(x, ("site", "blk"), route)

    def exchange(x):
        return lax.all_to_all(x, "blk", 0, 0, tiled=True, axis_index_groups=groups)

    def pick(a, b):
        return jnp.where(first, a, b)

    row = charge
    scale = jnp.broadcast_to(charge.astype(BF16), (8, chi))
    other_corner = swap_cores(corner[0])
    pair_corner = [pick(corner[0], other_corner), pick(other_corner, corner[0])]
    near = site_move(jnp.concatenate(pair_corner + [scale], axis=0), 1, False)
    to_row = near[pair_rows : pair_rows + 1].astype(jnp.int32)
    near = near[:pair_rows]

    def array(*shape, dtype=BF16):
        return jax.ShapeDtypeStruct(shape, dtype)

    edge_flat = edge[0].reshape(rows * depth, chi)
    part_left = contract_first(edge_flat, proj_left[0].reshape(rows * depth, chi))
    part_right = contract_first(edge_flat, proj_right[0].reshape(rows * depth, chi))
    other_part = swap_cores(pick(part_right, part_left).astype(BF16))
    part_bf = (pick(part_left, part_right) + other_part.astype(F32)).astype(BF16)
    packed = call(
        pack_kernel,
        array(chi, WIDE + FOLD),
        [VMEM] * 5 + [ANY] * 2,
        [pltpu.VMEM((chi, WIDE + FOLD), BF16), pltpu.VMEM((2, rows, chi), F32), pltpu.SemaphoreType.DMA((3,))],
        chi * chi * 8,
        6 << 20,
        HBM,
    )(part_left, part_right, other_part, row, to_row, cot_left[0], cot_right[0])
    got = exchange(packed.reshape(chips, pair_rows, WIDE + FOLD))
    summed, early = call(
        sum_kernel,
        (array(chips, pair_rows, WIDE), array(chips, pair_rows, FOLD)),
        [HBM],
        [
            pltpu.VMEM((chips, pair_rows, WIDE + FOLD), BF16),
            pltpu.VMEM((pair_rows, WIDE), BF16),
            pltpu.SemaphoreType.DMA((chips,)),
        ],
        0,
        3 << 20,
        (HBM, VMEM),
        63 << 20,
    )(got)
    enl = exchange(summed).reshape(chi, WIDE)

    rings = 2
    ring = chips // rings

    def turn(i, dy, dz):
        y, z, core = i // (2 * ring), i // 2 % ring, i % 2
        return (((y + dy) % rings) * ring + (z + dz) % ring) * 2 + core

    def ring_move(x, dy, dz):
        return lax.ppermute(x, "blk", [(i, turn(i, dy, dz)) for i in range(members)])

    near = jnp.concatenate([near, ring_move(near, 1, 0)], axis=0)
    up = down = near
    pieces = [near]
    for n in range(1, ring // 2 + 1):
        up = ring_move(up, 0, 1)
        pieces.append(up)
        if n < ring // 2:
            down = ring_move(down, 0, -1)
            pieces.append(down)
    near = call(weave_kernel, array(chi, chi), [ANY] * ring, [pltpu.SemaphoreType.DMA((chips,))], 0, 3 << 20, VMEM, 60 << 20)(*pieces)
    near_other = swap_cores(near)

    early_other = swap_cores(early)
    w_open, cot = call(
        start_kernel,
        (array(chi, WIDE), array(chi, FOLD)),
        [VMEM] * 3,
        [pltpu.VMEM((chi, FOLD), BF16)],
        0,
        1 << 20,
        (VMEM, VMEM),
    )(early, early_other, row)
    back1 = call(first_kernel, array(chi, FOLD), [VMEM] * 3, [], chi * chi * WIDE, 2 << 20)(w_open, enl, to_row)
    back1_at = site_move(back1, -1, False)
    back2 = call(
        second_kernel, array(chi, FOLD), [VMEM] * 5, [pltpu.VMEM((WIDE, chi), BF16)], chi * chi * WIDE, 2 << 20
    )(cot, back1_at, enl, row, to_row)
    back2_at = site_move(back2, -1, False)
    w2 = (cot.astype(F32) + back2_at.astype(F32)).astype(BF16)
    w2_other = swap_cores(w2)

    new_part = call(new_kernel, array(chi, FOLD), [VMEM] * 3, [], chi * chi * chi, 3 << 20)(near, part_bf, row)
    new_got = exchange(new_part.reshape(chips, pair_rows, FOLD))
    new_sum = call(total_kernel, array(pair_rows, FOLD, dtype=F32), [VMEM], [], 0, 1 << 18)(new_got)
    new_other = swap_cores(new_sum)
    new_left, new_right = call(
        open_kernel, (array(rows, chi), array(rows, chi)), [VMEM] * 3, [], 0, 1 << 17, (VMEM, VMEM)
    )(new_sum, new_other, row)

    flat = array(rows * depth, chi)
    grad_left, grad_right = call(
        grad_kernel,
        (flat, flat),
        [HBM] * 3 + [VMEM] * 3,
        [
            pltpu.VMEM((rows * depth, chi), BF16),
            pltpu.VMEM((2, chi, chi), BF16),
            pltpu.VMEM((FOLD, WIDE), BF16),
            pltpu.VMEM((chi, chi), BF16),
            pltpu.VMEM((SLOTS, STEP, chi), BF16),
            pltpu.SemaphoreType.DMA((rows * depth // STEP + 2,)),
            pltpu.SemaphoreType.DMA((SLOTS,)),
        ],
        4 * rows * depth * chi * chi,
        8 << 20,
        (HBM, HBM),
        62 << 20,
    )(edge_flat, near, near_other, w2, w2_other, row)
    return (
        new_left[None],
        new_right[None],
        grad_left.reshape(1, rows, depth, chi),
        grad_right.reshape(1, rows, depth, chi),
    )


def solution(mesh):
    row = P("site", "blk", None)
    flat = P("site", "blk", None, None)

    return jax.shard_map(
        body,
        mesh=mesh,
        in_specs=(row, flat, flat, flat, P("site", None), row, row),
        out_specs=(row, row, flat, flat),
        check_vma=False,
    )
```

```python
import jax
import jax.numpy as jnp
from jax import lax
from jax.experimental import pallas as pl
from jax.experimental.pallas import tpu as pltpu
from jax.sharding import PartitionSpec as P


SECTORS = 16
FOLD = 128
WIDE = 384
F32 = jnp.float32
BF16 = jnp.bfloat16
VMEM = pl.BlockSpec(memory_space=pltpu.VMEM)
ANY = pl.BlockSpec(memory_space=pl.ANY)
HBM = pl.BlockSpec(memory_space=pltpu.HBM)


def contract_first(left, right):
    return lax.dot_general(left, right, (((0,), (0,)), ((), ())), preferred_element_type=F32)


def contract_last(left, right):
    return lax.dot_general(left, right, (((1,), (1,)), ((), ())), preferred_element_type=F32)


def fold_lanes(x, width):
    pieces = [x[:, at : at + width] for at in range(0, x.shape[1], width)]
    total = pieces[0]
    for piece in pieces[1:]:
        total = total + piece
    return total


def near_tiles(i, tiles):
    return max(0, i - 1), min(tiles, i + 2)


def label_row(ref):
    return ref[...].astype(F32)


def column(row, i):
    return jnp.broadcast_to(row[:, FOLD * i : FOLD * (i + 1)], (FOLD, FOLD)).T


def lanes(q):
    return slice(FOLD * q, FOLD * (q + 1))


def pack_kernel(
    left_ref, right_ref, other_ref, row_ref, to_row_ref, cot_left_ref, cot_right_ref,
    out_ref, cot_ref, sems,
):
    chi = left_ref.shape[0]
    rows = cot_ref.shape[1]
    tiles = chi // FOLD
    wide = WIDE // FOLD
    blk = lax.axis_index("blk")
    copies = [
        pltpu.make_async_copy(ref, cot_ref.at[n], sems.at[n])
        for n, ref in enumerate((cot_left_ref, cot_right_ref))
    ]
    for copy in copies:
        copy.start()
    row, to_row = label_row(row_ref), label_row(to_row_ref)
    low, high = jnp.zeros_like(row), jnp.zeros_like(row)
    for n in range(SECTORS):
        member = to_row == float(n)
        least = jnp.min(jnp.where(member, row, float(SECTORS)), axis=1, keepdims=True)
        most = jnp.max(jnp.where(member, row, -1.0), axis=1, keepdims=True)
        low = low + jnp.where(member, least, 0.0)
        high = high + jnp.where(member, most, 0.0)

    def fold(own_ref):
        for i in range(tiles):
            at = lanes(i)
            low_col, high_col = column(low, i), column(high, i)
            totals = [None] * wide
            for q in range(tiles):
                part = own_ref[at, lanes(q)] + other_ref[at, lanes(q)].astype(F32)
                label = row[:, lanes(q)]
                part = jnp.where((label >= low_col) & (label <= high_col), part, 0.0)
                old = totals[q % wide]
                totals[q % wide] = part if old is None else old + part
            for q in range(wide):
                out_ref[at, lanes(q)] = totals[q].astype(BF16)

    @pl.when(lax.rem(blk, 2) == 0)
    def _():
        fold(left_ref)

    @pl.when(lax.rem(blk, 2) == 1)
    def _():
        fold(right_ref)

    position = lax.broadcasted_iota(jnp.int32, (rows, chi), 1)
    wanted = blk * rows + lax.broadcasted_iota(jnp.int32, (rows, chi), 0)
    own = jnp.sum(jnp.where(position == wanted, row, 0.0), axis=1, keepdims=True)
    mask = own == row
    for n, copy in enumerate(copies):
        copy.wait()
        cot = fold_lanes(jnp.where(mask, cot_ref[n], 0.0), FOLD).astype(BF16)
        for q in range(chi // (2 * rows)):
            at = 2 * rows * q + rows * n
            out_ref[at : at + rows, WIDE:] = cot


def sum_kernel(got_ref, out_ref, early_ref):
    total = got_ref[0, :, :WIDE].astype(F32)
    for q in range(1, got_ref.shape[0]):
        total = total + got_ref[q, :, :WIDE].astype(F32)
    out_ref[...] = jnp.broadcast_to(total.astype(BF16)[None], out_ref.shape)
    early_ref[...] = got_ref[:, :, WIDE:]


def pair_kernel(own_ref, other_ref, out_ref):
    rows = own_ref.shape[0]
    core = lax.rem(lax.axis_index("blk"), 2)

    @pl.when(core == 0)
    def _():
        out_ref[:rows, :] = own_ref[...]
        out_ref[rows : 2 * rows, :] = other_ref[...]

    @pl.when(core == 1)
    def _():
        out_ref[:rows, :] = other_ref[...]
        out_ref[rows : 2 * rows, :] = own_ref[...]


def start_kernel(early_ref, other_ref, row_ref, open_ref, cot_ref, w_ref):
    chips, pair_rows, _ = early_ref.shape
    rows = pair_rows // 2
    core = lax.rem(lax.axis_index("blk"), 2)

    @pl.when(core == 0)
    def _():
        for q in range(chips):
            w_ref[pair_rows * q : pair_rows * q + rows, :] = early_ref[q, :rows, :]
            w_ref[pair_rows * q + rows : pair_rows * (q + 1), :] = other_ref[q, :rows, :]

    @pl.when(core == 1)
    def _():
        for q in range(chips):
            w_ref[pair_rows * q : pair_rows * q + rows, :] = other_ref[q, rows:, :]
            w_ref[pair_rows * q + rows : pair_rows * (q + 1), :] = early_ref[q, rows:, :]

    row = label_row(row_ref)
    tiles = w_ref.shape[0] // FOLD
    wide = WIDE // FOLD
    cols = [column(row, i) for i in range(tiles)]
    for i in range(tiles):
        low, high = near_tiles(i, tiles)
        total = jnp.zeros((FOLD, FOLD), F32)
        for q in range(low, high):
            total = total + jnp.where(cols[q] == row[:, lanes(i)], w_ref[lanes(q), :].astype(F32), 0.0)
        cot_ref[lanes(i), :] = total.T.astype(BF16)
        w = w_ref[lanes(i), :].astype(F32)
        for q in range(wide):
            same = (cols[i] == row[:, lanes(q)]) | (cols[i] == row[:, lanes(wide + q)])
            open_ref[lanes(i), lanes(q)] = jnp.where(same, w, 0.0).astype(BF16)


def fold_tile(product, col, row, low, high):
    total = jnp.zeros((FOLD, FOLD), F32)
    for q in range(low, high):
        total = total + jnp.where(col == row[:, lanes(q)], product[:, lanes(q - low)], 0.0)
    return total.astype(BF16)


def new_kernel(*refs):
    *piece_refs, part_hbm, row_ref, turned_ref, out_ref, near_ref, part_ref, sems = refs
    ring = len(piece_refs)
    block = piece_refs[0].shape[0] // 2
    chip = lax.div(lax.axis_index("blk"), 2)
    y, z = lax.div(chip, ring), lax.rem(chip, ring)
    copies = [pltpu.make_async_copy(part_hbm, part_ref, sems.at[2 * ring])]
    for n, ref in enumerate(piece_refs):
        step = -((n + 1) // 2) if n % 2 else n // 2
        for half in range(2):
            source = lax.rem(y + half, 2) * ring + lax.rem(z + step + ring, ring)
            at = pl.multiple_of(source * block, 16)
            copies.append(
                pltpu.make_async_copy(
                    ref.at[pl.ds(block * half, block)], near_ref.at[pl.ds(at, block)], sems.at[2 * n + half]
                )
            )
    for copy in copies:
        copy.start()
    for copy in copies:
        copy.wait()
    tiles = near_ref.shape[0] // FOLD
    row = label_row(row_ref)
    for i in range(tiles):
        turned_ref[:, lanes(i)] = near_ref[lanes(i), :].astype(F32).T.astype(BF16)
    for i in range(tiles):
        low, high = near_tiles(i, tiles)
        product = jnp.dot(
            near_ref[lanes(i), :], part_ref[:, FOLD * low : FOLD * high], preferred_element_type=F32
        )
        out_ref[lanes(i), :] = fold_tile(product, column(row, i), row, low, high)


def total_kernel(got_ref, out_ref):
    total = got_ref[0].astype(F32)
    for q in range(1, got_ref.shape[0]):
        total = total + got_ref[q].astype(F32)
    out_ref[...] = total


def open_kernel(own_ref, other_ref, row_ref, left_ref, right_ref):
    rows, chi = left_ref.shape
    blk = lax.axis_index("blk")
    core = lax.rem(blk, 2)
    row = label_row(row_ref)
    position = lax.broadcasted_iota(jnp.int32, (rows, chi), 1)
    wanted = blk * rows + lax.broadcasted_iota(jnp.int32, (rows, chi), 0)
    mask = jnp.sum(jnp.where(position == wanted, row, 0.0), axis=1, keepdims=True) == row

    def put(out_ref, x):
        wide = jnp.concatenate([x] * (chi // FOLD), axis=1)
        out_ref[...] = jnp.where(mask, wide, 0.0).astype(BF16)

    @pl.when(core == 0)
    def _():
        put(left_ref, own_ref[:rows, :])
        put(right_ref, other_ref[:rows, :])

    @pl.when(core == 1)
    def _():
        put(right_ref, own_ref[rows:, :])
        put(left_ref, other_ref[rows:, :])


def first_kernel(open_ref, enl_ref, to_row_ref, out_ref):
    to_row = label_row(to_row_ref)
    tiles = out_ref.shape[0] // FOLD
    for i in range(tiles):
        low, high = near_tiles(i, tiles)
        back = contract_last(enl_ref[lanes(i), :], open_ref[FOLD * low : FOLD * high, :])
        out_ref[lanes(i), :] = fold_tile(back, column(to_row, i), to_row, low, high)


def second_kernel(cot_ref, back_ref, enl_ref, row_ref, to_row_ref, out_ref, open_ref):
    row, to_row = label_row(row_ref), label_row(to_row_ref)
    tiles = out_ref.shape[0] // FOLD
    wide = WIDE // FOLD
    for i in range(wide):
        halves = []
        for at in (lanes(i), lanes(wide + i)):
            w = (cot_ref[at, :].astype(F32) + back_ref[at, :].astype(F32)).astype(BF16)
            halves.append(w.astype(F32))
        cols = column(row, i), column(row, wide + i)
        for q in range(tiles):
            total = jnp.where(cols[0] == row[:, lanes(q)], halves[0], 0.0)
            total = total + jnp.where(cols[1] == row[:, lanes(q)], halves[1], 0.0)
            open_ref[lanes(i), lanes(q)] = total.astype(BF16)
    for i in range(tiles):
        low, high = near_tiles(i, tiles)
        back = jnp.dot(
            enl_ref[lanes(i), :], open_ref[:, FOLD * low : FOLD * high], preferred_element_type=F32
        )
        out_ref[lanes(i), :] = fold_tile(back, column(to_row, i), to_row, low, high)


SLOTS = 4
STEP = 384


def grad_kernel(
    edge_hbm, near_hbm, other_hbm, w_ref, w_other_ref, row_ref, left_ref, right_ref,
    edge_ref, near_ref, open_ref, mid_ref, stage_ref, in_sems, sems,
):
    core = lax.rem(lax.axis_index("blk"), 2)
    chi = near_ref.shape[1]
    tiles = chi // FOLD
    steps = edge_ref.shape[0] // STEP
    row = label_row(row_ref)
    near_copies = [
        pltpu.make_async_copy(ref, near_ref.at[n], in_sems.at[steps + n])
        for n, ref in enumerate((near_hbm, other_hbm))
    ]
    edge_copies = [
        pltpu.make_async_copy(
            edge_hbm.at[pl.ds(STEP * n, STEP)], edge_ref.at[pl.ds(STEP * n, STEP)], in_sems.at[n]
        )
        for n in range(steps)
    ]
    near_copies[0].start()
    for copy in edge_copies:
        copy.start()
    near_copies[1].start()
    for side, w in enumerate((w_ref, w_other_ref)):
        near_copies[side].wait()
        cols = [column(row, q) for q in range(tiles)]
        for i in range(0, tiles, 2):
            low, high = max(0, i - 1), min(tiles, i + 3)
            for half in range(2):
                x = w[lanes(i + half), :].astype(F32).T
                for q in range(low, high):
                    same = cols[q] == row[:, lanes(i + half)]
                    open_ref[lanes(q - low), lanes(half)] = jnp.where(same, x, 0.0).astype(BF16)
            mid_ref[:, FOLD * i : FOLD * (i + 2)] = jnp.dot(
                near_ref[side, :, FOLD * low : FOLD * high],
                open_ref[: FOLD * (high - low), :],
                preferred_element_type=F32,
            ).astype(BF16)
        for n in range(steps):
            at = side * steps + n
            slot = at % SLOTS
            rows = pl.ds(STEP * n, STEP)
            if side == 0:
                edge_copies[n].wait()
            if at >= SLOTS:
                pltpu.make_async_copy(stage_ref.at[slot], left_ref.at[rows], sems.at[slot]).wait()
            stage_ref[slot] = jnp.dot(
                edge_ref[STEP * n : STEP * (n + 1), :], mid_ref[...], preferred_element_type=F32
            ).astype(BF16)

            @pl.when(core == side)
            def _():
                pltpu.make_async_copy(stage_ref.at[slot], left_ref.at[rows], sems.at[slot]).start()

            @pl.when(core != side)
            def _():
                pltpu.make_async_copy(stage_ref.at[slot], right_ref.at[rows], sems.at[slot]).start()

    for slot in range(SLOTS):
        pltpu.make_async_copy(stage_ref.at[slot], left_ref.at[pl.ds(0, STEP)], sems.at[slot]).wait()


def call(kernel, out_shape, in_specs, scratch, flops, moved, out_specs=VMEM, limit=24 << 20):
    return pl.pallas_call(
        kernel,
        out_shape=out_shape,
        in_specs=in_specs,
        out_specs=out_specs,
        scratch_shapes=scratch,
        cost_estimate=pl.CostEstimate(flops=flops, bytes_accessed=moved, transcendentals=0),
        compiler_params=pltpu.CompilerParams(vmem_limit_bytes=limit),
    )


def body(corner, edge, proj_left, proj_right, charge, cot_left, cot_right):
    sites = lax.axis_size("site")
    members = lax.axis_size("blk")
    rows, chi = corner.shape[1], corner.shape[2]
    depth = edge.shape[2]
    chips = members // 2
    pair_rows = 2 * rows
    blk = lax.axis_index("blk")
    first = blk % 2 == 0
    groups = [[2 * q + core for q in range(chips)] for core in range(2)]

    def swap_cores(x):
        return lax.ppermute(x, "blk", [(i, i ^ 1) for i in range(members)])

    def site_move(x, distance, cross):
        route = []
        for s in range(sites):
            for i in range(members):
                target = i ^ 1 if cross else i
                sign = 1 if target % 2 == 0 else -1
                route.append((s * members + i, ((s + sign * distance) % sites) * members + target))
        return lax.ppermute(x, ("site", "blk"), route)

    def exchange(x):
        return lax.all_to_all(x, "blk", 0, 0, tiled=True, axis_index_groups=groups)

    def pick(a, b):
        return jnp.where(first, a, b)

    row = charge
    to_row = site_move(charge, 1, False)
    other_corner = swap_cores(corner[0])

    def array(*shape, dtype=BF16):
        return jax.ShapeDtypeStruct(shape, dtype)

    pair_corner = call(pair_kernel, array(pair_rows, chi), [VMEM] * 2, [], 0, 1 << 18)(
        corner[0], other_corner
    )
    near = site_move(pair_corner, 1, False)

    edge_flat = edge[0].reshape(rows * depth, chi)
    part_left = contract_first(edge_flat, proj_left[0].reshape(rows * depth, chi))
    part_right = contract_first(edge_flat, proj_right[0].reshape(rows * depth, chi))
    other_part = swap_cores(pick(part_right, part_left).astype(BF16))
    part_bf = (pick(part_left, part_right) + other_part.astype(F32)).astype(BF16)
    packed = call(
        pack_kernel,
        array(chi, WIDE + FOLD),
        [VMEM] * 5 + [ANY] * 2,
        [pltpu.VMEM((2, rows, chi), F32), pltpu.SemaphoreType.DMA((2,))],
        chi * chi * 8,
        6 << 20,
    )(part_left, part_right, other_part, row, to_row, cot_left[0], cot_right[0])
    got = exchange(packed.reshape(chips, pair_rows, WIDE + FOLD))
    summed, early = call(
        sum_kernel,
        (array(chips, pair_rows, WIDE), array(chips, pair_rows, FOLD)),
        [VMEM],
        [],
        0,
        3 << 20,
        (VMEM, VMEM),
    )(got)
    enl = exchange(summed).reshape(chi, WIDE)

    rings = 2
    ring = chips // rings

    def turn(i, dy, dz):
        y, z, core = i // (2 * ring), i // 2 % ring, i % 2
        return (((y + dy) % rings) * ring + (z + dz) % ring) * 2 + core

    def ring_move(x, dy, dz):
        return lax.ppermute(x, "blk", [(i, turn(i, dy, dz)) for i in range(members)])

    near = jnp.concatenate([near, ring_move(near, 1, 0)], axis=0)
    up = down = near
    pieces = [near]
    for n in range(1, ring // 2 + 1):
        up = ring_move(up, 0, 1)
        pieces.append(up)
        if n < ring // 2:
            down = ring_move(down, 0, -1)
            pieces.append(down)
    near, new_part = call(
        new_kernel,
        (array(chi, chi), array(chi, FOLD)),
        [ANY] * (ring + 1) + [VMEM],
        [pltpu.VMEM((chi, chi), BF16)] * 2 + [pltpu.SemaphoreType.DMA((chips + 1,))],
        chi * chi * chi,
        3 << 20,
        (VMEM, VMEM),
        60 << 20,
    )(*pieces, part_bf, row)
    near_other = swap_cores(near)

    early_other = swap_cores(early)
    w_open, cot = call(
        start_kernel,
        (array(chi, WIDE), array(chi, FOLD)),
        [VMEM] * 3,
        [pltpu.VMEM((chi, FOLD), BF16)],
        0,
        1 << 20,
        (VMEM, VMEM),
    )(early, early_other, row)
    back1 = call(first_kernel, array(chi, FOLD), [VMEM] * 3, [], chi * chi * WIDE, 2 << 20)(
        w_open, enl, to_row
    )
    back1_at = site_move(back1, -1, False)
    back2 = call(
        second_kernel, array(chi, FOLD), [VMEM] * 5, [pltpu.VMEM((WIDE, chi), BF16)], chi * chi * WIDE, 2 << 20
    )(cot, back1_at, enl, row, to_row)
    back2_at = site_move(back2, -1, False)
    w2 = (cot.astype(F32) + back2_at.astype(F32)).astype(BF16)
    w2_other = swap_cores(w2)

    new_got = exchange(new_part.reshape(chips, pair_rows, FOLD))
    new_sum = call(total_kernel, array(pair_rows, FOLD, dtype=F32), [VMEM], [], 0, 1 << 18)(new_got)
    new_other = swap_cores(new_sum)
    new_left, new_right = call(
        open_kernel, (array(rows, chi), array(rows, chi)), [VMEM] * 3, [], 0, 1 << 17, (VMEM, VMEM)
    )(new_sum, new_other, row)

    flat = array(rows * depth, chi)
    grad_left, grad_right = call(
        grad_kernel,
        (flat, flat),
        [HBM] * 3 + [VMEM] * 3,
        [
            pltpu.VMEM((rows * depth, chi), BF16),
            pltpu.VMEM((2, chi, chi), BF16),
            pltpu.VMEM((4 * FOLD, 2 * FOLD), BF16),
            pltpu.VMEM((chi, chi), BF16),
            pltpu.VMEM((SLOTS, STEP, chi), BF16),
            pltpu.SemaphoreType.DMA((rows * depth // STEP + 2,)),
            pltpu.SemaphoreType.DMA((SLOTS,)),
        ],
        4 * rows * depth * chi * chi,
        8 << 20,
        (HBM, HBM),
        60 << 20,
    )(edge_flat, near, near_other, w2, w2_other, row)
    return (
        new_left[None],
        new_right[None],
        grad_left.reshape(1, rows, depth, chi),
        grad_right.reshape(1, rows, depth, chi),
    )


def solution(mesh):
    row = P("site", "blk", None)
    flat = P("site", "blk", None, None)

    return jax.shard_map(
        body,
        mesh=mesh,
        in_specs=(row, flat, flat, flat, P("site", None), row, row),
        out_specs=(row, row, flat, flat),
        check_vma=False,
    )
```

```python
import jax
import jax.numpy as jnp
from jax import lax
from jax.experimental import pallas as pl
from jax.experimental.pallas import tpu as pltpu
from jax.sharding import PartitionSpec as P


SECTORS = 16
FOLD = 128
WIDE = 384
F32 = jnp.float32
BF16 = jnp.bfloat16
VMEM = pl.BlockSpec(memory_space=pltpu.VMEM)
ANY = pl.BlockSpec(memory_space=pl.ANY)
HBM = pl.BlockSpec(memory_space=pltpu.HBM)


def contract_first(left, right):
    return lax.dot_general(left, right, (((0,), (0,)), ((), ())), preferred_element_type=F32)


def contract_last(left, right):
    return lax.dot_general(left, right, (((1,), (1,)), ((), ())), preferred_element_type=F32)


def fold_lanes(x, width):
    pieces = [x[:, at : at + width] for at in range(0, x.shape[1], width)]
    total = pieces[0]
    for piece in pieces[1:]:
        total = total + piece
    return total


def near_tiles(i, tiles):
    return max(0, i - 1), min(tiles, i + 2)


def label_row(ref):
    return ref[...].astype(F32)


def column(row, i):
    return jnp.broadcast_to(row[:, FOLD * i : FOLD * (i + 1)], (FOLD, FOLD)).T


def lanes(q):
    return slice(FOLD * q, FOLD * (q + 1))


def pack_kernel(
    left_ref, right_ref, other_ref, row_ref, to_row_ref, cot_left_ref, cot_right_ref,
    out_ref, cot_ref, sems,
):
    chi = left_ref.shape[0]
    rows = cot_ref.shape[1]
    tiles = chi // FOLD
    wide = WIDE // FOLD
    blk = lax.axis_index("blk")
    copies = [
        pltpu.make_async_copy(ref, cot_ref.at[n], sems.at[n])
        for n, ref in enumerate((cot_left_ref, cot_right_ref))
    ]
    for copy in copies:
        copy.start()
    row, to_row = label_row(row_ref), label_row(to_row_ref)
    low, high = jnp.zeros_like(row), jnp.zeros_like(row)
    for n in range(SECTORS):
        member = to_row == float(n)
        least = jnp.min(jnp.where(member, row, float(SECTORS)), axis=1, keepdims=True)
        most = jnp.max(jnp.where(member, row, -1.0), axis=1, keepdims=True)
        low = low + jnp.where(member, least, 0.0)
        high = high + jnp.where(member, most, 0.0)

    def fold(own_ref):
        for i in range(tiles):
            at = lanes(i)
            low_col, high_col = column(low, i), column(high, i)
            totals = [None] * wide
            for q in range(tiles):
                part = own_ref[at, lanes(q)] + other_ref[at, lanes(q)].astype(F32)
                label = row[:, lanes(q)]
                part = jnp.where((label >= low_col) & (label <= high_col), part, 0.0)
                old = totals[q % wide]
                totals[q % wide] = part if old is None else old + part
            for q in range(wide):
                out_ref[at, lanes(q)] = totals[q].astype(BF16)

    @pl.when(lax.rem(blk, 2) == 0)
    def _():
        fold(left_ref)

    @pl.when(lax.rem(blk, 2) == 1)
    def _():
        fold(right_ref)

    position = lax.broadcasted_iota(jnp.int32, (rows, chi), 1)
    wanted = blk * rows + lax.broadcasted_iota(jnp.int32, (rows, chi), 0)
    own = jnp.sum(jnp.where(position == wanted, row, 0.0), axis=1, keepdims=True)
    mask = own == row
    for n, copy in enumerate(copies):
        copy.wait()
        cot = fold_lanes(jnp.where(mask, cot_ref[n], 0.0), FOLD).astype(BF16)
        for q in range(chi // (2 * rows)):
            at = 2 * rows * q + rows * n
            out_ref[at : at + rows, WIDE:] = cot


def sum_kernel(got_ref, out_ref, early_ref):
    total = got_ref[0, :, :WIDE].astype(F32)
    for q in range(1, got_ref.shape[0]):
        total = total + got_ref[q, :, :WIDE].astype(F32)
    out_ref[...] = jnp.broadcast_to(total.astype(BF16)[None], out_ref.shape)
    early_ref[...] = got_ref[:, :, WIDE:]


def pair_kernel(own_ref, other_ref, out_ref):
    rows = own_ref.shape[0]
    core = lax.rem(lax.axis_index("blk"), 2)

    @pl.when(core == 0)
    def _():
        out_ref[:rows, :] = own_ref[...]
        out_ref[rows : 2 * rows, :] = other_ref[...]

    @pl.when(core == 1)
    def _():
        out_ref[:rows, :] = other_ref[...]
        out_ref[rows : 2 * rows, :] = own_ref[...]


def start_kernel(early_ref, other_ref, row_ref, open_ref, cot_ref, w_ref):
    chips, pair_rows, _ = early_ref.shape
    rows = pair_rows // 2
    core = lax.rem(lax.axis_index("blk"), 2)

    @pl.when(core == 0)
    def _():
        for q in range(chips):
            w_ref[pair_rows * q : pair_rows * q + rows, :] = early_ref[q, :rows, :]
            w_ref[pair_rows * q + rows : pair_rows * (q + 1), :] = other_ref[q, :rows, :]

    @pl.when(core == 1)
    def _():
        for q in range(chips):
            w_ref[pair_rows * q : pair_rows * q + rows, :] = other_ref[q, rows:, :]
            w_ref[pair_rows * q + rows : pair_rows * (q + 1), :] = early_ref[q, rows:, :]

    row = label_row(row_ref)
    tiles = w_ref.shape[0] // FOLD
    wide = WIDE // FOLD
    cols = [column(row, i) for i in range(tiles)]
    for i in range(tiles):
        low, high = near_tiles(i, tiles)
        total = jnp.zeros((FOLD, FOLD), F32)
        for q in range(low, high):
            total = total + jnp.where(cols[q] == row[:, lanes(i)], w_ref[lanes(q), :].astype(F32), 0.0)
        cot_ref[lanes(i), :] = total.T.astype(BF16)
        w = w_ref[lanes(i), :].astype(F32)
        for q in range(wide):
            same = (cols[i] == row[:, lanes(q)]) | (cols[i] == row[:, lanes(wide + q)])
            open_ref[lanes(i), lanes(q)] = jnp.where(same, w, 0.0).astype(BF16)


def fold_tile(product, col, row, low, high):
    total = jnp.zeros((FOLD, FOLD), F32)
    for q in range(low, high):
        total = total + jnp.where(col == row[:, lanes(q)], product[:, lanes(q - low)], 0.0)
    return total.astype(BF16)


def new_kernel(*refs):
    *piece_refs, part_hbm, row_ref, turned_ref, out_ref, near_ref, part_ref, sems = refs
    ring = len(piece_refs)
    block = piece_refs[0].shape[0] // 2
    chip = lax.div(lax.axis_index("blk"), 2)
    y, z = lax.div(chip, ring), lax.rem(chip, ring)
    copies = [pltpu.make_async_copy(part_hbm, part_ref, sems.at[2 * ring])]
    for n, ref in enumerate(piece_refs):
        step = -((n + 1) // 2) if n % 2 else n // 2
        for half in range(2):
            source = lax.rem(y + half, 2) * ring + lax.rem(z + step + ring, ring)
            at = pl.multiple_of(source * block, 16)
            copies.append(
                pltpu.make_async_copy(
                    ref.at[pl.ds(block * half, block)], near_ref.at[pl.ds(at, block)], sems.at[2 * n + half]
                )
            )
    for copy in copies:
        copy.start()
    for copy in copies:
        copy.wait()
    tiles = near_ref.shape[0] // FOLD
    row = label_row(row_ref)
    for i in range(tiles):
        turned_ref[:, lanes(i)] = near_ref[lanes(i), :].astype(F32).T.astype(BF16)
    for i in range(tiles):
        low, high = near_tiles(i, tiles)
        product = jnp.dot(
            near_ref[lanes(i), :], part_ref[:, FOLD * low : FOLD * high], preferred_element_type=F32
        )
        out_ref[lanes(i), :] = fold_tile(product, column(row, i), row, low, high)


def open_kernel(got_ref, row_ref, left_ref, right_ref):
    rows, chi = left_ref.shape
    blk = lax.axis_index("blk")
    row = label_row(row_ref)
    position = lax.broadcasted_iota(jnp.int32, (rows, chi), 1)
    wanted = blk * rows + lax.broadcasted_iota(jnp.int32, (rows, chi), 0)
    mask = jnp.sum(jnp.where(position == wanted, row, 0.0), axis=1, keepdims=True) == row
    for side, out_ref in enumerate((left_ref, right_ref)):
        total = got_ref[side].astype(F32)
        for q in range(side + 2, got_ref.shape[0], 2):
            total = total + got_ref[q].astype(F32)
        wide = jnp.concatenate([total] * (chi // FOLD), axis=1)
        out_ref[...] = jnp.where(mask, wide, 0.0).astype(BF16)


def first_kernel(open_ref, enl_ref, to_row_ref, out_ref):
    to_row = label_row(to_row_ref)
    tiles = out_ref.shape[0] // FOLD
    for i in range(tiles):
        low, high = near_tiles(i, tiles)
        back = contract_last(enl_ref[lanes(i), :], open_ref[FOLD * low : FOLD * high, :])
        out_ref[lanes(i), :] = fold_tile(back, column(to_row, i), to_row, low, high)


def second_kernel(cot_ref, back_ref, enl_ref, row_ref, to_row_ref, out_ref, open_ref):
    row, to_row = label_row(row_ref), label_row(to_row_ref)
    tiles = out_ref.shape[0] // FOLD
    wide = WIDE // FOLD
    for i in range(wide):
        halves = []
        for at in (lanes(i), lanes(wide + i)):
            w = (cot_ref[at, :].astype(F32) + back_ref[at, :].astype(F32)).astype(BF16)
            halves.append(w.astype(F32))
        cols = column(row, i), column(row, wide + i)
        for q in range(tiles):
            total = jnp.where(cols[0] == row[:, lanes(q)], halves[0], 0.0)
            total = total + jnp.where(cols[1] == row[:, lanes(q)], halves[1], 0.0)
            open_ref[lanes(i), lanes(q)] = total.astype(BF16)
    for i in range(tiles):
        low, high = near_tiles(i, tiles)
        back = jnp.dot(
            enl_ref[lanes(i), :], open_ref[:, FOLD * low : FOLD * high], preferred_element_type=F32
        )
        out_ref[lanes(i), :] = fold_tile(back, column(to_row, i), to_row, low, high)


SLOTS = 4
STEP = 384


def grad_kernel(
    edge_hbm, near_hbm, other_hbm, w_ref, w_other_ref, row_ref, left_ref, right_ref,
    edge_ref, near_ref, open_ref, mid_ref, stage_ref, in_sems, sems,
):
    core = lax.rem(lax.axis_index("blk"), 2)
    chi = near_ref.shape[1]
    tiles = chi // FOLD
    steps = edge_ref.shape[0] // STEP
    row = label_row(row_ref)
    near_copies = [
        pltpu.make_async_copy(ref, near_ref.at[n], in_sems.at[steps + n])
        for n, ref in enumerate((near_hbm, other_hbm))
    ]
    edge_copies = [
        pltpu.make_async_copy(
            edge_hbm.at[pl.ds(STEP * n, STEP)], edge_ref.at[pl.ds(STEP * n, STEP)], in_sems.at[n]
        )
        for n in range(steps)
    ]
    near_copies[0].start()
    for copy in edge_copies:
        copy.start()
    near_copies[1].start()
    for side, w in enumerate((w_ref, w_other_ref)):
        near_copies[side].wait()
        cols = [column(row, q) for q in range(tiles)]
        for i in range(0, tiles, 2):
            low, high = max(0, i - 1), min(tiles, i + 3)
            for half in range(2):
                x = w[lanes(i + half), :].astype(F32).T
                for q in range(low, high):
                    same = cols[q] == row[:, lanes(i + half)]
                    open_ref[lanes(q - low), lanes(half)] = jnp.where(same, x, 0.0).astype(BF16)
            mid_ref[:, FOLD * i : FOLD * (i + 2)] = jnp.dot(
                near_ref[side, :, FOLD * low : FOLD * high],
                open_ref[: FOLD * (high - low), :],
                preferred_element_type=F32,
            ).astype(BF16)
        for n in range(steps):
            at = side * steps + n
            slot = at % SLOTS
            rows = pl.ds(STEP * n, STEP)
            if side == 0:
                edge_copies[n].wait()
            if at >= SLOTS:
                pltpu.make_async_copy(stage_ref.at[slot], left_ref.at[rows], sems.at[slot]).wait()
            stage_ref[slot] = jnp.dot(
                edge_ref[STEP * n : STEP * (n + 1), :], mid_ref[...], preferred_element_type=F32
            ).astype(BF16)

            @pl.when(core == side)
            def _():
                pltpu.make_async_copy(stage_ref.at[slot], left_ref.at[rows], sems.at[slot]).start()

            @pl.when(core != side)
            def _():
                pltpu.make_async_copy(stage_ref.at[slot], right_ref.at[rows], sems.at[slot]).start()

    for slot in range(SLOTS):
        pltpu.make_async_copy(stage_ref.at[slot], left_ref.at[pl.ds(0, STEP)], sems.at[slot]).wait()


def call(kernel, out_shape, in_specs, scratch, flops, moved, out_specs=VMEM, limit=24 << 20):
    return pl.pallas_call(
        kernel,
        out_shape=out_shape,
        in_specs=in_specs,
        out_specs=out_specs,
        scratch_shapes=scratch,
        cost_estimate=pl.CostEstimate(flops=flops, bytes_accessed=moved, transcendentals=0),
        compiler_params=pltpu.CompilerParams(vmem_limit_bytes=limit),
    )


def body(corner, edge, proj_left, proj_right, charge, cot_left, cot_right):
    sites = lax.axis_size("site")
    members = lax.axis_size("blk")
    rows, chi = corner.shape[1], corner.shape[2]
    depth = edge.shape[2]
    chips = members // 2
    pair_rows = 2 * rows
    blk = lax.axis_index("blk")
    first = blk % 2 == 0
    groups = [[2 * q + core for q in range(chips)] for core in range(2)]

    def swap_cores(x):
        return lax.ppermute(x, "blk", [(i, i ^ 1) for i in range(members)])

    def site_move(x, distance, cross):
        route = []
        for s in range(sites):
            for i in range(members):
                target = i ^ 1 if cross else i
                sign = 1 if target % 2 == 0 else -1
                route.append((s * members + i, ((s + sign * distance) % sites) * members + target))
        return lax.ppermute(x, ("site", "blk"), route)

    def exchange(x):
        return lax.all_to_all(x, "blk", 0, 0, tiled=True, axis_index_groups=groups)

    def pick(a, b):
        return jnp.where(first, a, b)

    row = charge
    to_row = site_move(charge, 1, False)
    other_corner = swap_cores(corner[0])

    def array(*shape, dtype=BF16):
        return jax.ShapeDtypeStruct(shape, dtype)

    pair_corner = call(pair_kernel, array(pair_rows, chi), [VMEM] * 2, [], 0, 1 << 18)(
        corner[0], other_corner
    )
    near = site_move(pair_corner, 1, False)

    edge_flat = edge[0].reshape(rows * depth, chi)
    part_left = contract_first(edge_flat, proj_left[0].reshape(rows * depth, chi))
    part_right = contract_first(edge_flat, proj_right[0].reshape(rows * depth, chi))
    other_part = swap_cores(pick(part_right, part_left).astype(BF16))
    part_bf = (pick(part_left, part_right) + other_part.astype(F32)).astype(BF16)
    packed = call(
        pack_kernel,
        array(chi, WIDE + FOLD),
        [VMEM] * 5 + [ANY] * 2,
        [pltpu.VMEM((2, rows, chi), F32), pltpu.SemaphoreType.DMA((2,))],
        chi * chi * 8,
        6 << 20,
    )(part_left, part_right, other_part, row, to_row, cot_left[0], cot_right[0])
    got = exchange(packed.reshape(chips, pair_rows, WIDE + FOLD))
    summed, early = call(
        sum_kernel,
        (array(chips, pair_rows, WIDE), array(chips, pair_rows, FOLD)),
        [VMEM],
        [],
        0,
        3 << 20,
        (VMEM, VMEM),
    )(got)
    enl = exchange(summed).reshape(chi, WIDE)

    rings = 2
    ring = chips // rings

    def turn(i, dy, dz):
        y, z, core = i // (2 * ring), i // 2 % ring, i % 2
        return (((y + dy) % rings) * ring + (z + dz) % ring) * 2 + core

    def ring_move(x, dy, dz):
        return lax.ppermute(x, "blk", [(i, turn(i, dy, dz)) for i in range(members)])

    near = jnp.concatenate([near, ring_move(near, 1, 0)], axis=0)
    up = down = near
    pieces = [near]
    for n in range(1, ring // 2 + 1):
        up = ring_move(up, 0, 1)
        pieces.append(up)
        if n < ring // 2:
            down = ring_move(down, 0, -1)
            pieces.append(down)
    near, new_part = call(
        new_kernel,
        (array(chi, chi), array(chi, FOLD)),
        [ANY] * (ring + 1) + [VMEM],
        [pltpu.VMEM((chi, chi), BF16)] * 2 + [pltpu.SemaphoreType.DMA((chips + 1,))],
        chi * chi * chi,
        3 << 20,
        (VMEM, VMEM),
        60 << 20,
    )(*pieces, part_bf, row)
    near_other = swap_cores(near)

    early_other = swap_cores(early)
    w_open, cot = call(
        start_kernel,
        (array(chi, WIDE), array(chi, FOLD)),
        [VMEM] * 3,
        [pltpu.VMEM((chi, FOLD), BF16)],
        0,
        1 << 20,
        (VMEM, VMEM),
    )(early, early_other, row)
    back1 = call(first_kernel, array(chi, FOLD), [VMEM] * 3, [], chi * chi * WIDE, 2 << 20)(
        w_open, enl, to_row
    )
    back1_at = site_move(back1, -1, False)
    back2 = call(
        second_kernel, array(chi, FOLD), [VMEM] * 5, [pltpu.VMEM((WIDE, chi), BF16)], chi * chi * WIDE, 2 << 20
    )(cot, back1_at, enl, row, to_row)
    back2_at = site_move(back2, -1, False)
    w2 = (cot.astype(F32) + back2_at.astype(F32)).astype(BF16)
    w2_other = swap_cores(w2)

    new_got = lax.all_to_all(new_part.reshape(members, rows, FOLD), "blk", 0, 0, tiled=True)
    new_left, new_right = call(
        open_kernel, (array(rows, chi), array(rows, chi)), [VMEM] * 2, [], 0, 1 << 18, (VMEM, VMEM)
    )(new_got, row)

    flat = array(rows * depth, chi)
    grad_left, grad_right = call(
        grad_kernel,
        (flat, flat),
        [HBM] * 3 + [VMEM] * 3,
        [
            pltpu.VMEM((rows * depth, chi), BF16),
            pltpu.VMEM((2, chi, chi), BF16),
            pltpu.VMEM((4 * FOLD, 2 * FOLD), BF16),
            pltpu.VMEM((chi, chi), BF16),
            pltpu.VMEM((SLOTS, STEP, chi), BF16),
            pltpu.SemaphoreType.DMA((rows * depth // STEP + 2,)),
            pltpu.SemaphoreType.DMA((SLOTS,)),
        ],
        4 * rows * depth * chi * chi,
        8 << 20,
        (HBM, HBM),
        60 << 20,
    )(edge_flat, near, near_other, w2, w2_other, row)
    return (
        new_left[None],
        new_right[None],
        grad_left.reshape(1, rows, depth, chi),
        grad_right.reshape(1, rows, depth, chi),
    )


def solution(mesh):
    row = P("site", "blk", None)
    flat = P("site", "blk", None, None)

    return jax.shard_map(
        body,
        mesh=mesh,
        in_specs=(row, flat, flat, flat, P("site", None), row, row),
        out_specs=(row, row, flat, flat),
        check_vma=False,
    )
```
